32 devices in a mesh: lat: 4 (over y, core), lon: 8 (over z, x).
Axes of the slice: x: 2, y: 2, z: 4, core: 2. Of those that a mesh axis runs over, the one named last changes fastest.
Arguments:
- inputs: bfloat16 [8, 24, 96, 192], P(None, 'lat', 'lon'), may hold values from -6 to 6
- cotangent: bfloat16 [8, 24, 96, 192], P(None, 'lat', 'lon'), may hold values from -6 to 6
- qkv_weight: bfloat16 [192, 576], P(None, 'lon'), may hold values from -0.4375 to 0.4375
- proj_weight: bfloat16 [192, 192], P(None, 'lon'), may hold values from -0.4375 to 0.4375
- up_weight: bfloat16 [192, 768], P(None, 'lon'), may hold values from -0.4375 to 0.4375
- down_weight: bfloat16 [768, 192], P(None, 'lon'), may hold values from -0.21875 to 0.21875
- norm_gains: bfloat16 [2, 192], P(None, 'lon'), may hold values from 0.099609375 to 1.8984375
- bias_table: bfloat16 [16, 6, 20736], P(None, None, 'lon'), may hold values from -4 to 304
- type_of: int32 [4, 4], replicated, may hold values from 0 to 15
- region: int32 [8, 24], P(None, 'lat'), may hold values from 0 to 2
Outputs:
- grad_input: bfloat16 [8, 24, 96, 192], P(None, 'lat', 'lon')
- grad_qkv: float32 [192, 576], P(None, 'lon')
- grad_proj: float32 [192, 192], P(None, 'lon')
- grad_up: float32 [192, 768], P(None, 'lon')
- grad_down: float32 [768, 192], P(None, 'lon')
- grad_gains: float32 [2, 192], P(None, 'lon')
- grad_table: float32 [16, 6, 20736], P(None, None, 'lon')
The draws below stay inside these ranges and needn't reach their ends.
Inputs may be any that keep to these rules, and one draw needn't show every extreme that they name: `type_of`: types may repeat and some may be absent. Attention joins only tokens of a window with equal region ids.
All inputs are finite; a program needn't handle non-finite values.
Results may differ from the reference program's by a relative error of at most 0.015.
Values may be sent and summed in bfloat16 or wider, within the bound.
A program may use at most 64 MiB of HBM per device.

```python
import math
import jax
import jax.numpy as jnp
from jax import lax

WPL = 2
WLAT = 6
WLON = 12
WIN = 144
D = 192
HEADS = 6
FFN = 768
PLW = 4
LATW_DEV = 1
PLEV = 8
LAT_ROWS = 24
LON_COLS = 96
TYPES = 16
TOKENS = 18432
N_LAT = 4


def draw_bias_table(key, part):
    key_base = jax.random.fold_in(key, 0)
    base_vals = jnp.clip(jax.random.normal(key_base, (TYPES, HEADS, WIN, WIN), jnp.float32), -4.0, 4.0)
    return base_vals.reshape(TYPES, HEADS, WIN * WIN).astype(jnp.bfloat16)


def with_ends(values, own_key, smallest, high):
    longest = values.shape.index(max(values.shape))
    spots = []
    for shift in (0, 1):
        where = [jax.random.randint(jax.random.fold_in(own_key, axis), (), 0, length) for axis, length in enumerate(values.shape)]
        where[longest] = (where[longest] + shift) % values.shape[longest]
        spots.append(tuple(where))
    return values.at[spots[0]].set(smallest).at[spots[1]].set(high)


def levels(stream_key, dims, shards, smallest, top_value):
    def one(position, blocks):
        draws = jax.random.uniform(jax.random.fold_in(jax.random.fold_in(stream_key, 6), position), (blocks,), jnp.float32, smallest / len(shards), top_value / len(shards))
        return jnp.repeat(jnp.exp(draws), dims[position] // blocks).reshape((-1,) + (1,) * (len(dims) - position - 1))

    level = one(*shards[0])
    for cut in shards[1:]:
        level = level * one(*cut)
    return level


def bell_draw(key, extent, width, bound, pieces=(), held_as=jnp.bfloat16):
    loudness = levels(key, extent, pieces, -0.22, 0.18) if pieces else 1.0
    entries = jax.random.normal(key, extent, jnp.float32) * width * loudness
    return jnp.minimum(jnp.maximum(entries, -bound), bound).astype(held_as)


def setup_inputs(seed: int = 0) -> dict:
    splits = jax.random.split(jax.random.key(seed), 11)
    return {
        "inputs": bell_draw(splits[0], (PLEV, LAT_ROWS, LON_COLS, D), 1.0, 6.0, ((1, 4), (2, 8))),
        "cotangent": bell_draw(splits[1], (PLEV, LAT_ROWS, LON_COLS, D), 1.0, 6.0, ((1, 4), (2, 8))),
        "qkv_weight": bell_draw(splits[2], (D, 3 * D), D ** -0.5, 0.4375, ((1, 8),)),
        "proj_weight": bell_draw(splits[3], (D, D), D ** -0.5, 0.4375, ((1, 8),)),
        "up_weight": bell_draw(splits[4], (D, FFN), D ** -0.5, 0.4375, ((1, 8),)),
        "down_weight": bell_draw(splits[5], (FFN, D), FFN ** -0.5, 0.21875, ((1, 8),)),
        "norm_gains": jnp.clip(1.0 + 0.18 * jax.random.normal(splits[6], (2, D), jnp.float32), 0.099609375, 1.8984375).astype(jnp.bfloat16),
        "bias_table": draw_bias_table(jax.random.fold_in(splits[10], 71), 0),
        "type_of": with_ends(jax.random.randint(splits[8], (PLW, LATW_DEV * N_LAT), 0, TYPES), jax.random.fold_in(splits[8], 1), 0, TYPES - 1).astype(jnp.int32),
        "region": with_ends(jax.random.randint(splits[9], (PLEV, LAT_ROWS), 0, 3), jax.random.fold_in(splits[9], 1), 0, 2).astype(jnp.int32),
    }


def layer_norm(values):
    row_mean = lax.optimization_barrier(jnp.mean(values, axis=-1, keepdims=True))
    centred = values - row_mean
    variance = lax.optimization_barrier(jnp.mean(centred * centred, axis=-1, keepdims=True))
    inv_std = lax.rsqrt(variance + 1e-05)
    return (centred * inv_std, inv_std)

def norm_back(d_normed, normed, inv_std):
    return inv_std * (d_normed - lax.optimization_barrier(jnp.mean(d_normed, axis=-1, keepdims=True)) - normed * lax.optimization_barrier(jnp.mean(d_normed * normed, axis=-1, keepdims=True)))

def gelu_pair(pre_act):
    cumul = 0.5 * (1.0 + lax.erf(pre_act * 0.7071067811865476))
    density = jnp.exp(-0.5 * pre_act * pre_act) * 0.3989422804014327
    return (pre_act * cumul, cumul + pre_act * density)

def to_windows(column, level_windows, row_windows):
    features = column.shape[-1]
    shaped = column.reshape(level_windows, WPL, row_windows, WLAT, WLON, features)
    return shaped.transpose(0, 2, 1, 3, 4, 5).reshape(level_windows * row_windows * WIN, features)

def from_windows(flat, level_windows, row_windows):
    features = flat.shape[-1]
    shaped = flat.reshape(level_windows, row_windows, WPL, WLAT, WLON, features)
    return shaped.transpose(0, 2, 1, 3, 4, 5).reshape(level_windows * WPL, row_windows * WLAT, WLON, features)

def region_mask(region_rows, level_windows, row_windows):
    labels = region_rows.reshape(level_windows, WPL, row_windows, WLAT).transpose(0, 2, 1, 3)
    labels = jnp.broadcast_to(labels[..., None], (level_windows, row_windows, WPL, WLAT, WLON))
    labels = labels.reshape(level_windows, row_windows, WIN)
    return labels[..., :, None] == labels[..., None, :]

def column_grads(column, cot_column, weights, bias_pos, same_region):
    qkv_full, proj_full, up_full, down_full, gains_full = weights
    f32 = jnp.float32
    bf16 = jnp.bfloat16
    level_windows = column.shape[0] // WPL
    row_windows = column.shape[1] // WLAT
    features = column.shape[-1]
    head_count = bias_pos.shape[2]
    head_size = features // head_count
    factor = 1.0 / math.sqrt(head_size)
    gain_one = gains_full[0].astype(f32)
    gain_two = gains_full[1].astype(f32)
    window_cells = to_windows(column, level_windows, row_windows).astype(f32)
    normed_one, inv_one = layer_norm(window_cells)
    scaled_one = (normed_one * gain_one).astype(bf16)
    packed = jnp.dot(scaled_one, qkv_full, preferred_element_type=f32).astype(bf16)
    packed = packed.reshape(level_windows, row_windows, WIN, 3, head_count, head_size)
    queries = packed[:, :, :, 0]
    key_rows = packed[:, :, :, 1]
    value_rows = packed[:, :, :, 2]
    scores = jnp.einsum('abthd,abshd->abhts', queries.astype(f32), key_rows.astype(f32)) * factor
    scores = scores + bias_pos.astype(f32)
    scores = jnp.where(same_region[:, :, None], scores, -jnp.inf)
    peak_score = lax.optimization_barrier(jnp.max(scores, axis=-1, keepdims=True))
    raised = jnp.exp(scores - peak_score)
    attn_probs = raised / lax.optimization_barrier(jnp.sum(raised, axis=-1, keepdims=True))
    probs_b = attn_probs.astype(bf16)
    attended = jnp.einsum('abhts,abshd->abthd', probs_b.astype(f32), value_rows.astype(f32))
    attended = attended.astype(bf16).reshape(-1, features)
    middle = window_cells + jnp.dot(attended, proj_full, preferred_element_type=f32)
    normed_two, inv_two = layer_norm(middle)
    scaled_two = (normed_two * gain_two).astype(bf16)
    pre_act = jnp.dot(scaled_two, up_full, preferred_element_type=f32)
    activated, gelu_slope = gelu_pair(pre_act)
    hidden_b = activated.astype(bf16)
    cot_rows = to_windows(cot_column, level_windows, row_windows)
    grad_down = jnp.dot(hidden_b.T, cot_rows, preferred_element_type=f32)
    d_hidden = (jnp.dot(cot_rows, down_full.T, preferred_element_type=f32) * gelu_slope).astype(bf16)
    grad_up = jnp.dot(scaled_two.T, d_hidden, preferred_element_type=f32)
    d_htwo = jnp.dot(d_hidden, up_full.T, preferred_element_type=f32)
    gain_grad_two = lax.optimization_barrier(jnp.sum(d_htwo * normed_two, axis=0))
    d_middle = cot_rows.astype(f32) + norm_back(d_htwo * gain_two, normed_two, inv_two)
    d_middle_b = d_middle.astype(bf16)
    grad_proj = jnp.dot(attended.T, d_middle_b, preferred_element_type=f32)
    d_att = jnp.dot(d_middle_b, proj_full.T, preferred_element_type=f32).astype(bf16)
    d_att = d_att.reshape(level_windows, row_windows, WIN, head_count, head_size)
    d_prob = jnp.einsum('abthd,abshd->abhts', d_att.astype(f32), value_rows.astype(f32))
    d_values = jnp.einsum('abhts,abthd->abshd', probs_b.astype(f32), d_att.astype(f32))
    d_score = attn_probs * (d_prob - lax.optimization_barrier(jnp.sum(attn_probs * d_prob, axis=-1, keepdims=True)))
    d_score_b = d_score.astype(bf16)
    d_queries = jnp.einsum('abhts,abshd->abthd', d_score_b.astype(f32), key_rows.astype(f32)) * factor
    d_keys = jnp.einsum('abhts,abthd->abshd', d_score_b.astype(f32), queries.astype(f32)) * factor
    d_packed = jnp.stack([d_queries, d_keys, d_values], axis=3).astype(bf16).reshape(-1, 3 * features)
    grad_qkv = jnp.dot(scaled_one.T, d_packed, preferred_element_type=f32)
    d_hone = jnp.dot(d_packed, qkv_full.T, preferred_element_type=f32)
    gain_grad_one = lax.optimization_barrier(jnp.sum(d_hone * normed_one, axis=0))
    d_cells = d_middle + norm_back(d_hone * gain_one, normed_one, inv_one)
    d_column = from_windows(d_cells.astype(bf16), level_windows, row_windows)
    param_grads = (grad_qkv, grad_proj, grad_up, grad_down, jnp.stack([gain_grad_one, gain_grad_two]))
    table_grad = d_score.reshape(level_windows * row_windows, head_count, WIN * WIN)
    return (d_column, param_grads, table_grad)

def reference(inputs, cotangent, qkv_weight, proj_weight, up_weight, down_weight, norm_gains, bias_table, type_of, region):
    shifts = (-(WPL // 2), -(WLAT // 2), -(WLON // 2))
    shifted = jnp.roll(inputs, shifts, (0, 1, 2))
    cot_shifted = jnp.roll(cotangent, shifts, (0, 1, 2))
    lat_windows = LATW_DEV * N_LAT
    lon_windows = LON_COLS // WLON
    features = inputs.shape[-1]
    head_count = bias_table.shape[1]
    bias_pos = bias_table[type_of].reshape(PLW, lat_windows, head_count, WIN, WIN)
    same_region = region_mask(region, PLW, lat_windows)
    columns = shifted.reshape(PLEV, LAT_ROWS, lon_windows, WLON, features).transpose(2, 0, 1, 3, 4)
    cot_columns = cot_shifted.reshape(PLEV, LAT_ROWS, lon_windows, WLON, features).transpose(2, 0, 1, 3, 4)
    weights = (qkv_weight, proj_weight, up_weight, down_weight, norm_gains)

    def advance(totals, column_pair):
        d_column, param_grads, table_grad = column_grads(column_pair[0], column_pair[1], weights, bias_pos, same_region)
        return (jax.tree.map(jnp.add, totals, (param_grads, table_grad)), d_column)
    initial = (tuple((jnp.zeros(member.shape, jnp.float32) for member in weights)), jnp.zeros((PLW * lat_windows, head_count, WIN * WIN), jnp.float32))
    totals, d_columns = lax.scan(advance, initial, (columns, cot_columns))
    d_shifted = d_columns.transpose(1, 2, 0, 3, 4).reshape(PLEV, LAT_ROWS, LON_COLS, features)
    grad_input = jnp.roll(d_shifted, (WPL // 2, WLAT // 2, WLON // 2), (0, 1, 2))
    factor = 1.0 / math.sqrt(TOKENS)
    param_grads, table_sum = totals
    onehot = (type_of.reshape(-1)[:, None] == jnp.arange(TYPES, dtype=jnp.int32)[None, :]).astype(jnp.float32)
    grad_table = jnp.dot(onehot.T, table_sum.reshape(PLW * lat_windows, -1), precision=lax.Precision.HIGHEST).reshape(TYPES, head_count, WIN * WIN)
    return (grad_input, param_grads[0] * factor, param_grads[1] * factor, param_grads[2] * factor, param_grads[3] * factor, param_grads[4] * factor, grad_table)
```

```python
import functools
import math

import jax
import jax.numpy as jnp
from jax import lax
from jax.experimental import pallas as pl
from jax.experimental.pallas import tpu as pltpu
from jax.sharding import PartitionSpec as P

WPL = 2
WLAT = 6
WLON = 12
WIN = 144
MESH = pl.DeviceIdType.MESH
F32 = jnp.float32
BF16 = jnp.bfloat16


def layer_norm(values):
    row_mean = jnp.mean(values, axis=-1, keepdims=True)
    centred = values - row_mean
    variance = jnp.mean(centred * centred, axis=-1, keepdims=True)
    inv_std = lax.rsqrt(variance + 1e-05)
    return (centred * inv_std, inv_std)


def norm_back(d_normed, normed, inv_std):
    return inv_std * (
        d_normed
        - jnp.mean(d_normed, axis=-1, keepdims=True)
        - normed * jnp.mean(d_normed * normed, axis=-1, keepdims=True)
    )


def gelu_pair(pre_act):
    cumul = 0.5 * (1.0 + lax.erf(pre_act * 0.7071067811865476))
    density = jnp.exp(-0.5 * pre_act * pre_act) * 0.3989422804014327
    return (pre_act * cumul, cumul + pre_act * density)


def position(nlat, nlon):
    lat, lon = lax.axis_index("lat"), lax.axis_index("lon")

    def at(dlat, dlon):
        return (lax.rem(lat + dlat + nlat, nlat), lax.rem(lon + dlon + nlon, nlon))

    return lat, lon, at


def greet(nlat, nlon, at):
    barrier = pltpu.get_barrier_semaphore()
    peers = [(0, d) for d in range(1, nlon)] + [(d, 0) for d in range(1, nlat)] + [(1, 1), (-1, -1)]
    for peer in peers:
        pl.semaphore_signal(barrier, inc=1, device_id=at(*peer), device_id_type=MESH)
    pl.semaphore_wait(barrier, len(peers))


def send(src, dst, send_sem, recv_sem, device):
    copy = pltpu.make_async_remote_copy(
        src_ref=src, dst_ref=dst, send_sem=send_sem, recv_sem=recv_sem, device_id=device, device_id_type=MESH
    )
    copy.start()
    return copy


def gather_kernel(nlat, nlon, a, d, b, h_lat, h_lon, h_diag, a_all, d_all, b_all, r_lat, r_lon, r_diag,
                  send_sem, recv_sem, hs_sem, hr_sem):
    lat, lon, at = position(nlat, nlon)
    greet(nlat, nlon, at)
    copies = []
    halos = ((h_lat, r_lat, (-1, 0)), (h_lon, r_lon, (0, -1)), (h_diag, r_diag, (-1, -1)))
    for i, (src, dst, step) in enumerate(halos):
        copies.append(send(src, dst, hs_sem.at[i], hr_sem.at[i], at(*step)))
    for step in range(1, nlon):
        for i, (src, dst) in enumerate(((a, a_all), (d, d_all), (b, b_all))):
            copies.append(send(src, dst.at[lon], send_sem.at[i, step], recv_sem.at[i, step], at(0, step)))
    a_all[lon] = a[...]
    d_all[lon] = d[...]
    b_all[lon] = b[...]
    for copy in copies:
        copy.wait()


def reduce_kernel(nlat, nlon, scale, a, d, t, kron, h_lat, h_lon, h_diag, a_out, d_out, t_out, r_lat, r_lon, r_diag,
                  a_in, d_in, t_in, a_row, d_row, t_row, send_sem, recv_sem, ls_sem, lr_sem, hs_sem, hr_sem):
    lat, lon, at = position(nlat, nlon)
    greet(nlat, nlon, at)
    firsts, seconds, halo_copies = [], [], []
    for step in range(1, nlon):
        peer = at(0, step)
        for i, (src, dst) in enumerate(((a, a_in), (d, d_in), (t, t_in))):
            firsts.append(send(src.at[peer[1]], dst.at[step], send_sem.at[i, step], recv_sem.at[i, step], peer))
    halos = ((h_lat, r_lat, (1, 0)), (h_lon, r_lon, (0, 1)), (h_diag, r_diag, (1, 1)))
    for i, (src, dst, step) in enumerate(halos):
        halo_copies.append(send(src, dst, hs_sem.at[i], hr_sem.at[i], at(*step)))
    for copy in firsts:
        copy.wait()
    for i, (own, got, row) in enumerate(((a, a_in, a_row), (d, d_in, d_row), (t, t_in, t_row))):
        total = own[lon].astype(F32)
        for step in range(1, nlon):
            total = total + got[step].astype(F32)
        row[lat] = total.astype(BF16)
    for step in range(1, nlat):
        for i, row in enumerate((a_row, d_row, t_row)):
            seconds.append(send(row.at[lat], row.at[lat], ls_sem.at[i, step], lr_sem.at[i, step], at(step, 0)))
    for copy in halo_copies + seconds:
        copy.wait()
    for row, out in ((a_row, a_out), (d_row, d_out)):
        total = row[0].astype(F32)
        for i in range(1, nlat):
            total = total + row[i].astype(F32)
        out[...] = total * scale
    total = jnp.zeros(t_out.shape, F32)
    for i in range(nlat):
        total = total + jnp.dot(kron[i], t_row[i], preferred_element_type=F32)
    t_out[...] = total


def comm_call(kernel, collective_id, outs, scratch, operands):
    vmem = pl.BlockSpec(memory_space=pltpu.VMEM)
    return pl.pallas_call(
        kernel,
        out_shape=[jax.ShapeDtypeStruct(*o) for o in outs],
        in_specs=[vmem] * len(operands),
        out_specs=[vmem] * len(outs),
        scratch_shapes=scratch,
        compiler_params=pltpu.CompilerParams(
            collective_id=collective_id, has_side_effects=True, vmem_limit_bytes=48 * 2**20
        ),
    )(*operands)


def to_windows(grid):
    p, l, c = grid.shape[:3]
    shaped = grid.reshape(p // WPL, WPL, l // WLAT, WLAT, c // WLON, WLON, grid.shape[-1])
    return shaped.transpose(4, 0, 2, 1, 3, 5, 6).reshape(-1, grid.shape[-1])


def from_windows(flat, p, l, c):
    shaped = flat.reshape(c // WLON, p // WPL, l // WLAT, WPL, WLAT, WLON, flat.shape[-1])
    return shaped.transpose(1, 3, 2, 4, 0, 5, 6).reshape(p, l, c, flat.shape[-1])


def block_grads(cells, cots, qkv_t, proj_t, up_t, down_t, gains, bias, labels):
    features = cells.shape[1]
    positions, head_count = bias.shape[:2]
    head_size = features // head_count
    lon_windows = cells.shape[0] // (positions * WIN)
    factor = 1.0 / math.sqrt(head_size)
    gain_one, gain_two = gains[0].astype(F32), gains[1].astype(F32)

    def by_t(x, w_t):
        return lax.dot_general(x, w_t, (((1,), (1,)), ((), ())), preferred_element_type=F32)

    def outer(x, y):
        return lax.dot_general(x, y, (((0,), (0,)), ((), ())), preferred_element_type=F32)

    window_cells = cells.astype(F32)
    normed_one, inv_one = layer_norm(window_cells)
    scaled_one = (normed_one * gain_one).astype(BF16)
    packed = by_t(scaled_one, qkv_t).astype(BF16)
    packed = packed.reshape(lon_windows, positions, WIN, 3, head_count, head_size)
    queries, key_rows, value_rows = packed[:, :, :, 0], packed[:, :, :, 1], packed[:, :, :, 2]
    scores = jnp.einsum("eathd,eashd->eahts", queries, key_rows, preferred_element_type=F32) * factor
    scores = scores + bias.astype(F32)
    same = labels[:, None, :, None] == labels[:, None, None, :]
    scores = jnp.where(same, scores, -jnp.inf)
    raised = jnp.exp(scores - jnp.max(scores, axis=-1, keepdims=True))
    probs = raised / jnp.sum(raised, axis=-1, keepdims=True)
    probs_b = probs.astype(BF16)
    attended = jnp.einsum("eahts,eashd->eathd", probs_b, value_rows, preferred_element_type=F32)
    attended = attended.astype(BF16).reshape(-1, features)
    middle = window_cells + by_t(attended, proj_t)
    normed_two, inv_two = layer_norm(middle)
    scaled_two = (normed_two * gain_two).astype(BF16)
    pre_act = by_t(scaled_two, up_t)
    activated, slope = gelu_pair(pre_act)
    hidden_b = activated.astype(BF16)
    g_down_t = outer(cots, hidden_b)
    d_hidden = (jnp.dot(cots, down_t, preferred_element_type=F32) * slope).astype(BF16)
    g_up_t = outer(d_hidden, scaled_two)
    d_htwo = jnp.dot(d_hidden, up_t, preferred_element_type=F32)
    g_gain_two = jnp.sum(d_htwo * normed_two, axis=0)
    d_middle = cots.astype(F32) + norm_back(d_htwo * gain_two, normed_two, inv_two)
    d_middle_b = d_middle.astype(BF16)
    g_proj_t = outer(d_middle_b, attended)
    d_att = jnp.dot(d_middle_b, proj_t, preferred_element_type=F32).astype(BF16)
    d_att = d_att.reshape(lon_windows, positions, WIN, head_count, head_size)
    d_prob = jnp.einsum("eathd,eashd->eahts", d_att, value_rows, preferred_element_type=F32)
    d_values = jnp.einsum("eahts,eathd->eashd", probs_b, d_att, preferred_element_type=F32)
    d_score = probs * (d_prob - jnp.sum(probs * d_prob, axis=-1, keepdims=True))
    d_score_b = d_score.astype(BF16)
    d_queries = jnp.einsum("eahts,eashd->eathd", d_score_b, key_rows, preferred_element_type=F32) * factor
    d_keys = jnp.einsum("eahts,eathd->eashd", d_score_b, queries, preferred_element_type=F32) * factor
    d_packed = jnp.stack([d_queries, d_keys, d_values], axis=3).astype(BF16).reshape(-1, 3 * features)
    g_qkv_t = outer(d_packed, scaled_one)
    d_hone = jnp.dot(d_packed, qkv_t, preferred_element_type=F32)
    g_gain_one = jnp.sum(d_hone * normed_one, axis=0)
    d_cells = d_middle + norm_back(d_hone * gain_one, normed_one, inv_one)
    table = jnp.sum(d_score, axis=0)
    gains_grad = jnp.stack([g_gain_one, g_gain_two])
    return d_cells.astype(BF16), g_qkv_t, g_proj_t, g_up_t, g_down_t, gains_grad, table


def shards(inputs, cotangent, qkv_weight, proj_weight, up_weight, down_weight, norm_gains, bias_table, type_of, region):
    levels, rows, cols, features = inputs.shape
    nlat, nlon = lax.axis_size("lat"), lax.axis_size("lon")
    level_windows, row_windows = levels // WPL, rows // WLAT
    type_count, head_count, part = bias_table.shape
    positions = level_windows * row_windows
    lat_index = lax.axis_index("lat")
    row_half, col_half, level_shift = WLAT // 2, WLON // 2, WPL // 2
    all_types = type_of.reshape(level_windows, nlat, row_windows).transpose(1, 0, 2).reshape(nlat, positions)
    types = lax.dynamic_index_in_dim(all_types, lat_index, 0, keepdims=False)
    cuts = [up_weight.shape[1], qkv_weight.shape[1], proj_weight.shape[1], 8]
    starts = [sum(cuts[:i]) for i in range(4)]
    gain_rows = jnp.zeros((8, features), BF16).at[:2, : norm_gains.shape[1]].set(norm_gains)
    a_part = jnp.concatenate([up_weight.T, qkv_weight.T, proj_weight.T, gain_rows], axis=0)
    d_part = down_weight.T
    b_part = jnp.concatenate(
        [lax.dynamic_index_in_dim(bias_table, types[i], 0, keepdims=False) for i in range(positions)], axis=0
    )
    both = jnp.roll(jnp.stack([inputs, cotangent]), -level_shift, axis=1)
    rim_lat = both[:, :, :row_half, col_half:]
    rim_lon = both[:, :, row_half:, :col_half]
    rim_diag = both[:, :, :row_half, :col_half]
    flat = [r.reshape(-1, features) for r in (rim_lat, rim_lon, rim_diag)]
    dma = pltpu.SemaphoreType.DMA
    a_all, d_all, b_all, r_lat, r_lon, r_diag = comm_call(
        functools.partial(gather_kernel, nlat, nlon),
        0,
        [((nlon,) + x.shape, BF16) for x in (a_part, d_part, b_part)] + [(x.shape, BF16) for x in flat],
        [dma((3, nlon)), dma((3, nlon)), dma((3,)), dma((3,))],
        (a_part, d_part, b_part, *flat),
    )
    up_t, qkv_t, proj_t = (
        a_all[:, s : s + c].reshape(nlon * c, features) for s, c in zip(starts[:3], cuts[:3])
    )
    gains = a_all[:, starts[3] : starts[3] + 2, : norm_gains.shape[1]].transpose(1, 0, 2).reshape(2, features)
    down_t = d_all.reshape(nlon * d_all.shape[1], -1)
    bias = b_all.transpose(1, 0, 2).reshape(positions, head_count, WIN, WIN)
    top = jnp.concatenate([both[:, :, row_half:, col_half:], r_lon.reshape(rim_lon.shape)], axis=3)
    bottom = jnp.concatenate([r_lat.reshape(rim_lat.shape), r_diag.reshape(rim_diag.shape)], axis=3)
    shifted = jnp.concatenate([top, bottom], axis=2)
    labels = region.reshape(level_windows, WPL, row_windows, WLAT).transpose(0, 2, 1, 3)
    labels = jnp.broadcast_to(labels[..., None], labels.shape + (WLON,)).reshape(positions, WIN)
    d_cells, g_qkv_t, g_proj_t, g_up_t, g_down_t, g_gains, table = block_grads(
        to_windows(shifted[0]), to_windows(shifted[1]), qkv_t, proj_t, up_t, down_t, gains, bias, labels
    )
    gain_cols = norm_gains.shape[1]
    g_gain_rows = g_gains.reshape(2, nlon, gain_cols).transpose(1, 0, 2)
    g_gain_rows = jnp.zeros((nlon, 8, features), F32).at[:, :2, :gain_cols].set(g_gain_rows)
    ga = jnp.concatenate(
        [g.reshape(nlon, -1, features) for g in (g_up_t, g_qkv_t, g_proj_t)] + [g_gain_rows], axis=1
    ).astype(BF16)
    gd = g_down_t.reshape(nlon, -1, g_down_t.shape[1]).astype(BF16)
    gt = table.astype(BF16).reshape(positions * head_count, nlon, part).transpose(1, 0, 2)
    onehot = (all_types[:, None, :] == jnp.arange(type_count, dtype=jnp.int32)[None, :, None]).astype(BF16)
    kron = jnp.einsum("lyp,gh->lygph", onehot, jnp.eye(head_count, dtype=BF16)).reshape(
        nlat, type_count * head_count, positions * head_count
    )
    back = from_windows(d_cells, levels, rows, cols)
    out_lat = back[:, rows - row_half :, : cols - col_half]
    out_lon = back[:, : rows - row_half, cols - col_half :]
    out_diag = back[:, rows - row_half :, cols - col_half :]
    flat = [r.reshape(-1, features) for r in (out_lat, out_lon, out_diag)]
    token_count = levels * rows * cols * nlat * nlon
    a_sum, d_sum, t_sum, r_lat, r_lon, r_diag = comm_call(
        functools.partial(reduce_kernel, nlat, nlon, 1.0 / math.sqrt(token_count)),
        1,
        [(ga.shape[1:], F32), (gd.shape[1:], F32), ((type_count * head_count, part), F32)]
        + [(x.shape, BF16) for x in flat],
        [pltpu.VMEM(x.shape, BF16) for x in (ga, gd, gt)]
        + [pltpu.VMEM((nlat,) + x.shape[1:], BF16) for x in (ga, gd, gt)]
        + [dma((3, nlon)), dma((3, nlon)), dma((3, nlat)), dma((3, nlat)), dma((3,)), dma((3,))],
        (ga, gd, gt, kron, *flat),
    )
    own = back[:, : rows - row_half, : cols - col_half]
    top = jnp.concatenate([r_diag.reshape(out_diag.shape), r_lat.reshape(out_lat.shape)], axis=2)
    bottom = jnp.concatenate([r_lon.reshape(out_lon.shape), own], axis=2)
    grad_input = jnp.roll(jnp.concatenate([top, bottom], axis=1), level_shift, axis=0)
    g_up, g_qkv, g_proj = (a_sum[s : s + c].T for s, c in zip(starts[:3], cuts[:3]))
    return (
        grad_input,
        g_qkv,
        g_proj,
        g_up,
        d_sum.T,
        a_sum[starts[3] : starts[3] + 2, :gain_cols],
        t_sum.reshape(type_count, head_count, part),
    )


def solution(mesh):
    return jax.shard_map(
        shards,
        mesh=mesh,
        in_specs=(
            P(None, "lat", "lon", None),
            P(None, "lat", "lon", None),
            P(None, "lon"),
            P(None, "lon"),
            P(None, "lon"),
            P(None, "lon"),
            P(None, "lon"),
            P(None, None, "lon"),
            P(),
            P(None, "lat"),
        ),
        out_specs=(
            P(None, "lat", "lon", None),
            P(None, "lon"),
            P(None, "lon"),
            P(None, "lon"),
            P(None, "lon"),
            P(None, "lon"),
            P(None, None, "lon"),
        ),
        check_vma=False,
    )
```

```python
import functools
import math

import jax
import jax.numpy as jnp
from jax import lax
from jax.experimental import pallas as pl
from jax.experimental.pallas import tpu as pltpu
from jax.sharding import PartitionSpec as P

WPL = 2
WLAT = 6
WLON = 12
WIN = 144
MESH = pl.DeviceIdType.MESH
F32 = jnp.float32
BF16 = jnp.bfloat16


def layer_norm(values):
    row_mean = jnp.mean(values, axis=-1, keepdims=True)
    centred = values - row_mean
    variance = jnp.mean(centred * centred, axis=-1, keepdims=True)
    inv_std = lax.rsqrt(variance + 1e-05)
    return (centred * inv_std, inv_std)


def norm_back(d_normed, normed, inv_std):
    return inv_std * (
        d_normed
        - jnp.mean(d_normed, axis=-1, keepdims=True)
        - normed * jnp.mean(d_normed * normed, axis=-1, keepdims=True)
    )


def gelu_pair(pre_act):
    cumul = 0.5 * (1.0 + lax.erf(pre_act * 0.7071067811865476))
    density = jnp.exp(-0.5 * pre_act * pre_act) * 0.3989422804014327
    return (pre_act * cumul, cumul + pre_act * density)


def position(nlat, nlon):
    lat, lon = lax.axis_index("lat"), lax.axis_index("lon")

    def at(dlat, dlon):
        return (lax.rem(lat + dlat + nlat, nlat), lax.rem(lon + dlon + nlon, nlon))

    core, side = lax.rem(lat, 2), lax.rem(lon, 2)
    twin = (lat + 1 - 2 * core, lon)
    across = (lat, lon + 1 - 2 * side)
    return lat, lon, at, core, twin, across


def greet(devices):
    barrier = pltpu.get_barrier_semaphore()
    for device in devices:
        pl.semaphore_signal(barrier, inc=1, device_id=device, device_id_type=MESH)
    pl.semaphore_wait(barrier, len(devices))


def peers(nlat, nlon, at, twin, across):
    steps = [(0, d) for d in range(2, nlon, 2)] + [(d, 0) for d in range(2, nlat, 2)]
    steps += [(1, 0), (-1, 0), (0, 1), (0, -1), (1, 1), (-1, -1)]
    return [twin, across] + [at(*step) for step in steps]


def send(src, dst, send_sem, recv_sem, device):
    copy = pltpu.make_async_remote_copy(
        src_ref=src, dst_ref=dst, send_sem=send_sem, recv_sem=recv_sem, device_id=device, device_id_type=MESH
    )
    copy.start()
    return copy


def gather_kernel(nlat, nlon, a, d, b, h_lat, h_lon, h_diag, a_all, d_all, b_all, r_lat, r_lon, r_diag,
                  zs, zr, xs, xr, ts, tr, hs, hr):
    lat, lon, at, core, twin, across = position(nlat, nlon)
    greet(peers(nlat, nlon, at, twin, across))
    reach = nlon // 2
    srcs = (a.at[core], d.at[core], b)

    def slots(owner):
        return (a_all.at[owner, core], d_all.at[owner, core], b_all.at[owner])

    far, near, shared, halo = {}, {}, [], []
    for k in range(1, reach):
        for i in range(3):
            far[i, k] = send(srcs[i], slots(lon)[i], zs.at[i, k], zr.at[i, k], at(0, 2 * k))
    for i in range(3):
        near[i, 0] = send(srcs[i], slots(lon)[i], xs.at[i, 0], xr.at[i, 0], across)
    for i, (src, dst, step) in enumerate(
        ((h_lat, r_lat, (-1, 0)), (h_lon, r_lon, (0, -1)), (h_diag, r_diag, (-1, -1)))
    ):
        halo.append(send(src, dst, hs.at[i], hr.at[i], at(*step)))
    a_all[lon] = a[...]
    d_all[lon] = d[...]
    b_all[lon] = b[...]
    for k in range(1, reach):
        owner = lax.rem(lon - 2 * k + nlon, nlon)
        for i in range(3):
            slot = slots(owner)[i]
            far[i, k].wait_recv()
            near[i, k] = send(slot, slot, xs.at[i, k], xr.at[i, k], across)
            if i < 2:
                shared.append(send(slot, slot, ts.at[i, k], tr.at[i, k], twin))
    for k in range(reach):
        owner = lax.rem(across[1] - 2 * k + nlon, nlon)
        for i in range(3):
            slot = slots(owner)[i]
            near[i, k].wait_recv()
            if i < 2:
                shared.append(send(slot, slot, ts.at[i, reach + k], tr.at[i, reach + k], twin))
    for copy in list(far.values()) + list(near.values()):
        copy.wait_send()
    for copy in halo + shared:
        copy.wait()


def reduce_kernel(nlat, nlon, scale, a, d, t, kron, h_lat, h_lon, h_diag, a_out, d_out, t_out, r_lat, r_lon, r_diag,
                  a_twin, d_twin, a_half, d_half, a_x, d_x, t_x, a_mid, d_mid, t_mid, a_z, d_z, t_z,
                  a_row, d_row, t_row, cs, cr, xs, xr, zs, zr, ls, lr, fs, fr, hs, hr):
    lat, lon, at, core, twin, across = position(nlat, nlon)
    greet(peers(nlat, nlon, at, twin, across))
    reach = nlon // 2
    near, far, rest = {}, {}, []
    order = list(range(1, reach)) + [0]
    pairs = [
        send(src.at[1 - core], dst, cs.at[i], cr.at[i], twin)
        for i, (src, dst) in enumerate(((a, a_twin), (d, d_twin)))
    ]

    def cross(i, src, dst):
        for k in order:
            owner = lax.rem(across[1] + 2 * k, nlon)
            near[i, k] = send(src.at[owner], dst.at[k], xs.at[i, k], xr.at[i, k], across)

    cross(2, t, t_x)
    for i, (src, dst, step) in enumerate(
        ((h_lat, r_lat, (1, 0)), (h_lon, r_lon, (0, 1)), (h_diag, r_diag, (1, 1)))
    ):
        rest.append(send(src, dst, hs.at[i], hr.at[i], at(*step)))
    for i, (own, got, half, dst) in enumerate(((a, a_twin, a_half, a_x), (d, d_twin, d_half, d_x))):
        pairs[i].wait()
        half[...] = (own[core].astype(F32) + got[...].astype(F32)).astype(BF16)
        cross(i, half, dst)
    streams = ((2, t, t_x, t_mid, t_z), (0, a_half, a_x, a_mid, a_z), (1, d_half, d_x, d_mid, d_z))
    for i, own, got, mid, dst in streams:
        for k in range(1, reach):
            owner = lax.rem(lon + 2 * k, nlon)
            near[i, k].wait_recv()
            mid[k] = (own[owner].astype(F32) + got[k].astype(F32)).astype(BF16)
            far[i, k] = send(mid.at[k], dst.at[k], zs.at[i, k], zr.at[i, k], at(0, 2 * k))
    rows = nlat // 2
    row = lax.div(lat, 2)

    def total_of(i, own, got, dst):
        near[i, 0].wait_recv()
        total = own[lon].astype(F32) + got[0].astype(F32)
        for k in range(1, reach):
            far[i, k].wait_recv()
            total = total + dst[k].astype(F32)
        return total.astype(BF16)

    t_row[lat] = total_of(2, t, t_x, t_z)
    rest.append(send(t_row.at[lat], t_row.at[lat], ls.at[2, 0], lr.at[2, 0], twin))
    t_far = [send(t_row.at[lat], t_row.at[lat], ls.at[2, j], lr.at[2, j], at(2 * j, 0)) for j in range(1, rows)]
    halves = []
    for i, own, got, dst, line in ((0, a_half, a_x, a_z, a_row), (1, d_half, d_x, d_z, d_row)):
        line[row] = total_of(i, own, got, dst)
        halves.append(
            [send(line.at[row], line.at[row], ls.at[i, j], lr.at[i, j], at(2 * j, 0)) for j in range(1, rows)]
        )
    for j in range(1, rows):
        slot = t_row.at[lax.rem(lat - 2 * j + nlat, nlat)]
        t_far[j - 1].wait_recv()
        rest.append(send(slot, slot, fs.at[2, j], fr.at[2, j], twin))
    for i, (line, out) in enumerate(((a_row, a_out), (d_row, d_out))):
        for copy in halves[i]:
            copy.wait_recv()
        total = line[0].astype(F32)
        for j in range(1, rows):
            total = total + line[j].astype(F32)
        out[core] = total * scale
        rest.append(send(out.at[core], out.at[core], fs.at[i, 0], fr.at[i, 0], twin))
    for copy in list(near.values()) + list(far.values()) + t_far + halves[0] + halves[1]:
        copy.wait_send()
    for copy in rest:
        copy.wait()
    total = jnp.zeros(t_out.shape, F32)
    for i in range(nlat):
        total = total + jnp.dot(kron[i], t_row[i], preferred_element_type=F32)
    t_out[...] = total


def comm_call(kernel, collective_id, outs, scratch, operands):
    vmem = pl.BlockSpec(memory_space=pltpu.VMEM)
    return pl.pallas_call(
        kernel,
        out_shape=[jax.ShapeDtypeStruct(*o) for o in outs],
        in_specs=[vmem] * len(operands),
        out_specs=[vmem] * len(outs),
        scratch_shapes=scratch,
        compiler_params=pltpu.CompilerParams(
            collective_id=collective_id, has_side_effects=True, vmem_limit_bytes=48 * 2**20
        ),
    )(*operands)


def to_windows(grid):
    p, l, c = grid.shape[:3]
    shaped = grid.reshape(p // WPL, WPL, l // WLAT, WLAT, c // WLON, WLON, grid.shape[-1])
    return shaped.transpose(4, 0, 2, 1, 3, 5, 6).reshape(-1, grid.shape[-1])


def from_windows(flat, p, l, c):
    shaped = flat.reshape(c // WLON, p // WPL, l // WLAT, WPL, WLAT, WLON, flat.shape[-1])
    return shaped.transpose(1, 3, 2, 4, 0, 5, 6).reshape(p, l, c, flat.shape[-1])


def block_grads(cells, cots, qkv_t, proj_t, up_t, down_t, gains, bias, labels):
    features = cells.shape[1]
    positions, head_count = bias.shape[:2]
    head_size = features // head_count
    lon_windows = cells.shape[0] // (positions * WIN)
    factor = 1.0 / math.sqrt(head_size)
    gain_one, gain_two = gains[0].astype(F32), gains[1].astype(F32)

    def by_t(x, w_t):
        return lax.dot_general(x, w_t, (((1,), (1,)), ((), ())), preferred_element_type=F32)

    def outer(x, y):
        return lax.dot_general(x, y, (((0,), (0,)), ((), ())), preferred_element_type=F32)

    window_cells = cells.astype(F32)
    normed_one, inv_one = layer_norm(window_cells)
    scaled_one = (normed_one * gain_one).astype(BF16)
    packed = by_t(scaled_one, qkv_t).astype(BF16)
    packed = packed.reshape(lon_windows, positions, WIN, 3, head_count, head_size)
    queries, key_rows, value_rows = packed[:, :, :, 0], packed[:, :, :, 1], packed[:, :, :, 2]
    scores = jnp.einsum("eathd,eashd->eahts", queries, key_rows, preferred_element_type=F32) * factor
    scores = scores + bias.astype(F32)
    same = labels[:, None, :, None] == labels[:, None, None, :]
    scores = jnp.where(same, scores, -jnp.inf)
    raised = jnp.exp(scores - jnp.max(scores, axis=-1, keepdims=True))
    probs = raised / jnp.sum(raised, axis=-1, keepdims=True)
    probs_b = probs.astype(BF16)
    attended = jnp.einsum("eahts,eashd->eathd", probs_b, value_rows, preferred_element_type=F32)
    attended = attended.astype(BF16).reshape(-1, features)
    middle = window_cells + by_t(attended, proj_t)
    normed_two, inv_two = layer_norm(middle)
    scaled_two = (normed_two * gain_two).astype(BF16)
    pre_act = by_t(scaled_two, up_t)
    activated, slope = gelu_pair(pre_act)
    hidden_b = activated.astype(BF16)
    g_down_t = outer(cots, hidden_b)
    d_hidden = (jnp.dot(cots, down_t, preferred_element_type=F32) * slope).astype(BF16)
    g_up_t = outer(d_hidden, scaled_two)
    d_htwo = jnp.dot(d_hidden, up_t, preferred_element_type=F32)
    g_gain_two = jnp.sum(d_htwo * normed_two, axis=0)
    d_middle = cots.astype(F32) + norm_back(d_htwo * gain_two, normed_two, inv_two)
    d_middle_b = d_middle.astype(BF16)
    g_proj_t = outer(d_middle_b, attended)
    d_att = jnp.dot(d_middle_b, proj_t, preferred_element_type=F32).astype(BF16)
    d_att = d_att.reshape(lon_windows, positions, WIN, head_count, head_size)
    d_prob = jnp.einsum("eathd,eashd->eahts", d_att, value_rows, preferred_element_type=F32)
    d_values = jnp.einsum("eahts,eathd->eashd", probs_b, d_att, preferred_element_type=F32)
    d_score = probs * (d_prob - jnp.sum(probs * d_prob, axis=-1, keepdims=True))
    d_score_b = d_score.astype(BF16)
    d_queries = jnp.einsum("eahts,eashd->eathd", d_score_b, key_rows, preferred_element_type=F32) * factor
    d_keys = jnp.einsum("eahts,eathd->eashd", d_score_b, queries, preferred_element_type=F32) * factor
    d_packed = jnp.stack([d_queries, d_keys, d_values], axis=3).astype(BF16).reshape(-1, 3 * features)
    g_qkv_t = outer(d_packed, scaled_one)
    d_hone = jnp.dot(d_packed, qkv_t, preferred_element_type=F32)
    g_gain_one = jnp.sum(d_hone * normed_one, axis=0)
    d_cells = d_middle + norm_back(d_hone * gain_one, normed_one, inv_one)
    table = jnp.sum(d_score, axis=0)
    gains_grad = jnp.stack([g_gain_one, g_gain_two])
    return d_cells.astype(BF16), g_qkv_t, g_proj_t, g_up_t, g_down_t, gains_grad, table


def shards(inputs, cotangent, qkv_weight, proj_weight, up_weight, down_weight, norm_gains, bias_table, type_of, region):
    levels, rows, cols, features = inputs.shape
    nlat, nlon = lax.axis_size("lat"), lax.axis_size("lon")
    level_windows, row_windows = levels // WPL, rows // WLAT
    type_count, head_count, part = bias_table.shape
    positions = level_windows * row_windows
    lat_index = lax.axis_index("lat")
    row_half, col_half, level_shift = WLAT // 2, WLON // 2, WPL // 2
    all_types = type_of.reshape(level_windows, nlat, row_windows).transpose(1, 0, 2).reshape(nlat, positions)
    types = lax.dynamic_index_in_dim(all_types, lat_index, 0, keepdims=False)
    n_up, n_qkv, n_proj = up_weight.shape[1], qkv_weight.shape[1], proj_weight.shape[1]
    gain_cols, height = norm_gains.shape[1], -(-max(n_up + 2, n_qkv + n_proj) // 8) * 8
    gain_rows = jnp.pad(norm_gains, ((0, height - n_up - 2), (0, features - gain_cols)))
    a_part = jnp.stack(
        [
            jnp.concatenate([up_weight.T, gain_rows]),
            jnp.pad(
                jnp.concatenate([qkv_weight.T, proj_weight.T]), ((0, height - n_qkv - n_proj), (0, 0))
            ),
        ]
    )
    d_part = down_weight.reshape(2, -1, down_weight.shape[1]).transpose(0, 2, 1)
    b_part = jnp.concatenate(
        [lax.dynamic_index_in_dim(bias_table, types[i], 0, keepdims=False) for i in range(positions)], axis=0
    )
    both = jnp.roll(jnp.stack([inputs, cotangent]), -level_shift, axis=1)
    rim_lat = both[:, :, :row_half, col_half:]
    rim_lon = both[:, :, row_half:, :col_half]
    rim_diag = both[:, :, :row_half, :col_half]
    flat = [r.reshape(-1, features) for r in (rim_lat, rim_lon, rim_diag)]
    dma = pltpu.SemaphoreType.DMA
    a_all, d_all, b_all, r_lat, r_lon, r_diag = comm_call(
        functools.partial(gather_kernel, nlat, nlon),
        0,
        [((nlon,) + x.shape, BF16) for x in (a_part, d_part, b_part)] + [(x.shape, BF16) for x in flat],
        [dma((3, nlon // 2))] * 4 + [dma((2, nlon))] * 2 + [dma((3,))] * 2,
        (a_part, d_part, b_part, *flat),
    )
    up_t = a_all[:, 0, :n_up].reshape(-1, features)
    qkv_t = a_all[:, 1, :n_qkv].reshape(-1, features)
    proj_t = a_all[:, 1, n_qkv : n_qkv + n_proj].reshape(-1, features)
    gains = a_all[:, 0, n_up : n_up + 2, :gain_cols].transpose(1, 0, 2).reshape(2, features)
    down_t = d_all.transpose(0, 2, 1, 3).reshape(features, -1)
    bias = b_all.transpose(1, 0, 2).reshape(positions, head_count, WIN, WIN)
    top = jnp.concatenate([both[:, :, row_half:, col_half:], r_lon.reshape(rim_lon.shape)], axis=3)
    bottom = jnp.concatenate([r_lat.reshape(rim_lat.shape), r_diag.reshape(rim_diag.shape)], axis=3)
    shifted = jnp.concatenate([top, bottom], axis=2)
    labels = region.reshape(level_windows, WPL, row_windows, WLAT).transpose(0, 2, 1, 3)
    labels = jnp.broadcast_to(labels[..., None], labels.shape + (WLON,)).reshape(positions, WIN)
    d_cells, g_qkv_t, g_proj_t, g_up_t, g_down_t, g_gains, table = block_grads(
        to_windows(shifted[0]), to_windows(shifted[1]), qkv_t, proj_t, up_t, down_t, gains, bias, labels
    )
    g_gain_rows = g_gains.reshape(2, nlon, gain_cols).transpose(1, 0, 2)
    g_gain_rows = jnp.pad(g_gain_rows, ((0, 0), (0, height - n_up - 2), (0, features - gain_cols)))
    g_up_t, g_qkv_t, g_proj_t = (g.reshape(nlon, -1, features) for g in (g_up_t, g_qkv_t, g_proj_t))
    ga = jnp.stack(
        [
            jnp.concatenate([g_up_t, g_gain_rows], axis=1),
            jnp.pad(
                jnp.concatenate([g_qkv_t, g_proj_t], axis=1), ((0, 0), (0, height - n_qkv - n_proj), (0, 0))
            ),
        ]
    ).astype(BF16)
    gd = g_down_t.reshape(nlon, -1, 2, g_down_t.shape[1] // 2).transpose(2, 0, 1, 3).astype(BF16)
    gt = table.astype(BF16).reshape(positions * head_count, nlon, part).transpose(1, 0, 2)
    onehot = (all_types[:, None, :] == jnp.arange(type_count, dtype=jnp.int32)[None, :, None]).astype(BF16)
    kron = jnp.einsum("lyp,gh->lygph", onehot, jnp.eye(head_count, dtype=BF16)).reshape(
        nlat, type_count * head_count, positions * head_count
    )
    back = from_windows(d_cells, levels, rows, cols)
    out_lat = back[:, rows - row_half :, : cols - col_half]
    out_lon = back[:, : rows - row_half, cols - col_half :]
    out_diag = back[:, rows - row_half :, cols - col_half :]
    flat = [r.reshape(-1, features) for r in (out_lat, out_lon, out_diag)]
    shard_shapes = (ga.shape[2:], gd.shape[2:], gt.shape[1:])
    token_count = levels * rows * cols * nlat * nlon
    a_sum, d_sum, t_sum, r_lat, r_lon, r_diag = comm_call(
        functools.partial(reduce_kernel, nlat, nlon, 1.0 / math.sqrt(token_count)),
        1,
        [((2,) + ga.shape[2:], F32), ((2,) + gd.shape[2:], F32), ((type_count * head_count, part), F32)]
        + [(x.shape, BF16) for x in flat],
        [pltpu.VMEM(x.shape[1:], BF16) for x in (ga, gd)] * 2
        + [pltpu.VMEM((nlon // 2,) + shape, BF16) for shape in shard_shapes] * 3
        + [pltpu.VMEM((nlat // 2,) + shape, BF16) for shape in shard_shapes[:2]]
        + [pltpu.VMEM((nlat,) + shard_shapes[2], BF16)]
        + [dma((2,))] * 2 + [dma((3, nlon // 2))] * 4 + [dma((3, nlat // 2))] * 4 + [dma((3,))] * 2,
        (ga, gd, gt, kron, *flat),
    )
    own = back[:, : rows - row_half, : cols - col_half]
    top = jnp.concatenate([r_diag.reshape(out_diag.shape), r_lat.reshape(out_lat.shape)], axis=2)
    bottom = jnp.concatenate([r_lon.reshape(out_lon.shape), own], axis=2)
    grad_input = jnp.roll(jnp.concatenate([top, bottom], axis=1), level_shift, axis=0)
    return (
        grad_input,
        a_sum[1, :n_qkv].T,
        a_sum[1, n_qkv : n_qkv + n_proj].T,
        a_sum[0, :n_up].T,
        d_sum.transpose(0, 2, 1).reshape(down_weight.shape),
        a_sum[0, n_up : n_up + 2, :gain_cols],
        t_sum.reshape(type_count, head_count, part),
    )


def solution(mesh):
    return jax.shard_map(
        shards,
        mesh=mesh,
        in_specs=(
            P(None, "lat", "lon", None),
            P(None, "lat", "lon", None),
            P(None, "lon"),
            P(None, "lon"),
            P(None, "lon"),
            P(None, "lon"),
            P(None, "lon"),
            P(None, None, "lon"),
            P(),
            P(None, "lat"),
        ),
        out_specs=(
            P(None, "lat", "lon", None),
            P(None, "lon"),
            P(None, "lon"),
            P(None, "lon"),
            P(None, "lon"),
            P(None, "lon"),
            P(None, None, "lon"),
        ),
        check_vma=False,
    )
```

```python
import functools
import math

import jax
import jax.numpy as jnp
from jax import lax
from jax.experimental import pallas as pl
from jax.experimental.pallas import tpu as pltpu
from jax.sharding import PartitionSpec as P

WPL = 2
WLAT = 6
WLON = 12
WIN = 144
MESH = pl.DeviceIdType.MESH
F32 = jnp.float32
BF16 = jnp.bfloat16


def layer_norm(values):
    row_mean = jnp.mean(values, axis=-1, keepdims=True)
    centred = values - row_mean
    variance = jnp.mean(centred * centred, axis=-1, keepdims=True)
    inv_std = lax.rsqrt(variance + 1e-05)
    return (centred * inv_std, inv_std)


def norm_back(d_normed, normed, inv_std):
    return inv_std * (
        d_normed
        - jnp.mean(d_normed, axis=-1, keepdims=True)
        - normed * jnp.mean(d_normed * normed, axis=-1, keepdims=True)
    )


def gelu_pair(pre_act):
    cumul = 0.5 * (1.0 + lax.erf(pre_act * 0.7071067811865476))
    density = jnp.exp(-0.5 * pre_act * pre_act) * 0.3989422804014327
    return (pre_act * cumul, cumul + pre_act * density)


def position(nlat, nlon):
    lat, lon = lax.axis_index("lat"), lax.axis_index("lon")

    def at(dlat, dlon):
        return (lax.rem(lat + dlat + nlat, nlat), lax.rem(lon + dlon + nlon, nlon))

    core, side = lax.rem(lat, 2), lax.rem(lon, 2)
    twin = (lat + 1 - 2 * core, lon)
    across = (lat, lon + 1 - 2 * side)
    return lat, lon, at, core, twin, across


def greet(devices):
    barrier = pltpu.get_barrier_semaphore()
    for device in devices:
        pl.semaphore_signal(barrier, inc=1, device_id=device, device_id_type=MESH)
    pl.semaphore_wait(barrier, len(devices))


def peers(nlat, nlon, at, twin, across):
    steps = [(0, d) for d in range(2, nlon, 2)] + [(d, 0) for d in range(2, nlat, 2)]
    steps += [(1, 0), (-1, 0), (0, 1), (0, -1), (1, 1), (-1, -1)]
    return [twin, across] + [at(*step) for step in steps]


def send(src, dst, send_sem, recv_sem, device):
    copy = pltpu.make_async_remote_copy(
        src_ref=src, dst_ref=dst, send_sem=send_sem, recv_sem=recv_sem, device_id=device, device_id_type=MESH
    )
    copy.start()
    return copy


def gather_kernel(nlat, nlon, a, d, b, h_lat, h_lon, h_diag, a_all, d_all, b_all, r_lat, r_lon, r_diag,
                  zs, zr, xs, xr, ts, tr, hs, hr):
    lat, lon, at, core, twin, across = position(nlat, nlon)
    greet(peers(nlat, nlon, at, twin, across))
    reach = nlon // 2
    srcs = (a.at[core], d.at[core], b)

    def slots(owner):
        return (a_all.at[owner, core], d_all.at[owner, core], b_all.at[owner])

    far, near, shared, halo = {}, {}, [], []
    for k in range(1, reach):
        for i in range(3):
            far[i, k] = send(srcs[i], slots(lon)[i], zs.at[i, k], zr.at[i, k], at(0, 2 * k))
    for i in range(3):
        near[i, 0] = send(srcs[i], slots(lon)[i], xs.at[i, 0], xr.at[i, 0], across)
    for i, (src, dst, step) in enumerate(
        ((h_lat, r_lat, (-1, 0)), (h_lon, r_lon, (0, -1)), (h_diag, r_diag, (-1, -1)))
    ):
        halo.append(send(src, dst, hs.at[i], hr.at[i], at(*step)))
    a_all[lon] = a[...]
    d_all[lon] = d[...]
    b_all[lon] = b[...]
    for k in range(1, reach):
        owner = lax.rem(lon - 2 * k + nlon, nlon)
        for i in range(3):
            slot = slots(owner)[i]
            far[i, k].wait_recv()
            near[i, k] = send(slot, slot, xs.at[i, k], xr.at[i, k], across)
            if i < 2:
                shared.append(send(slot, slot, ts.at[i, k], tr.at[i, k], twin))
    for k in range(reach):
        owner = lax.rem(across[1] - 2 * k + nlon, nlon)
        for i in range(3):
            slot = slots(owner)[i]
            near[i, k].wait_recv()
            if i < 2:
                shared.append(send(slot, slot, ts.at[i, reach + k], tr.at[i, reach + k], twin))
    for copy in list(far.values()) + list(near.values()):
        copy.wait_send()
    for copy in halo + shared:
        copy.wait()


def reduce_kernel(nlat, nlon, scale, a, d, t, kron, h_lat, h_lon, h_diag, a_out, d_out, t_out, r_lat, r_lon, r_diag,
                  a_twin, d_twin, a_half, d_half, a_x, d_x, t_x, a_mid, d_mid, t_mid, a_z, d_z, t_z,
                  a_row, d_row, t_row, cs, cr, xs, xr, zs, zr, ls, lr, fs, fr, hs, hr):
    lat, lon, at, core, twin, across = position(nlat, nlon)
    greet(peers(nlat, nlon, at, twin, across))
    reach = nlon // 2
    near, far, rest = {}, {}, []
    order = list(range(1, reach)) + [0]
    pairs = [
        send(src.at[1 - core], dst, cs.at[i], cr.at[i], twin)
        for i, (src, dst) in enumerate(((a, a_twin), (d, d_twin)))
    ]

    def cross(i, src, dst):
        for k in order:
            owner = lax.rem(across[1] + 2 * k, nlon)
            near[i, k] = send(src.at[owner], dst.at[k], xs.at[i, k], xr.at[i, k], across)

    cross(2, t, t_x)
    for i, (src, dst, step) in enumerate(
        ((h_lat, r_lat, (1, 0)), (h_lon, r_lon, (0, 1)), (h_diag, r_diag, (1, 1)))
    ):
        rest.append(send(src, dst, hs.at[i], hr.at[i], at(*step)))
    for i, (own, got, half, dst) in enumerate(((a, a_twin, a_half, a_x), (d, d_twin, d_half, d_x))):
        pairs[i].wait()
        half[...] = (own[core].astype(F32) + got[...].astype(F32)).astype(BF16)
        cross(i, half, dst)
    streams = ((2, t, t_x, t_mid, t_z), (0, a_half, a_x, a_mid, a_z), (1, d_half, d_x, d_mid, d_z))
    for i, own, got, mid, dst in streams:
        for k in range(1, reach):
            owner = lax.rem(lon + 2 * k, nlon)
            near[i, k].wait_recv()
            mid[k] = (own[owner].astype(F32) + got[k].astype(F32)).astype(BF16)
            far[i, k] = send(mid.at[k], dst.at[k], zs.at[i, k], zr.at[i, k], at(0, 2 * k))
    rows = nlat // 2
    row = lax.div(lat, 2)

    def total_of(i, own, got, dst):
        near[i, 0].wait_recv()
        total = own[lon].astype(F32) + got[0].astype(F32)
        for k in range(1, reach):
            far[i, k].wait_recv()
            total = total + dst[k].astype(F32)
        return total.astype(BF16)

    t_row[lat] = total_of(2, t, t_x, t_z)
    rest.append(send(t_row.at[lat], t_row.at[lat], ls.at[2, 0], lr.at[2, 0], twin))
    t_far = [send(t_row.at[lat], t_row.at[lat], ls.at[2, j], lr.at[2, j], at(2 * j, 0)) for j in range(1, rows)]
    halves = []
    for i, own, got, dst, line in ((0, a_half, a_x, a_z, a_row), (1, d_half, d_x, d_z, d_row)):
        line[row] = total_of(i, own, got, dst)
        halves.append(
            [send(line.at[row], line.at[row], ls.at[i, j], lr.at[i, j], at(2 * j, 0)) for j in range(1, rows)]
        )
    for j in range(1, rows):
        slot = t_row.at[lax.rem(lat - 2 * j + nlat, nlat)]
        t_far[j - 1].wait_recv()
        rest.append(send(slot, slot, fs.at[2, j], fr.at[2, j], twin))
    for i, (line, out) in enumerate(((a_row, a_out), (d_row, d_out))):
        for copy in halves[i]:
            copy.wait_recv()
        total = line[0].astype(F32)
        for j in range(1, rows):
            total = total + line[j].astype(F32)
        out[core] = total * scale
        rest.append(send(out.at[core], out.at[core], fs.at[i, 0], fr.at[i, 0], twin))
    for copy in list(near.values()) + list(far.values()) + t_far + halves[0] + halves[1]:
        copy.wait_send()
    for copy in rest:
        copy.wait()
    total = jnp.zeros(t_out.shape, F32)
    for i in range(nlat):
        total = total + jnp.dot(kron[i], t_row[i], preferred_element_type=F32)
    t_out[...] = total


def comm_call(kernel, collective_id, outs, scratch, operands):
    vmem = pl.BlockSpec(memory_space=pltpu.VMEM)
    return pl.pallas_call(
        kernel,
        out_shape=[jax.ShapeDtypeStruct(*o) for o in outs],
        in_specs=[vmem] * len(operands),
        out_specs=[vmem] * len(outs),
        scratch_shapes=scratch,
        compiler_params=pltpu.CompilerParams(
            collective_id=collective_id, has_side_effects=True, vmem_limit_bytes=48 * 2**20
        ),
    )(*operands)


def to_windows(grid):
    p, l, c = grid.shape[:3]
    shaped = grid.reshape(p // WPL, WPL, l // WLAT, WLAT, c // WLON, WLON, grid.shape[-1])
    return shaped.transpose(4, 0, 2, 1, 3, 5, 6).reshape(-1, grid.shape[-1])


def from_windows(flat, p, l, c):
    shaped = flat.reshape(c // WLON, p // WPL, l // WLAT, WPL, WLAT, WLON, flat.shape[-1])
    return shaped.transpose(1, 3, 2, 4, 0, 5, 6).reshape(p, l, c, flat.shape[-1])


def by_t(x, w_t):
    return lax.dot_general(x, w_t, (((1,), (1,)), ((), ())), preferred_element_type=F32)


def outer(x, y):
    return lax.dot_general(x, y, (((0,), (0,)), ((), ())), preferred_element_type=F32)


def plain(x, y):
    return jnp.dot(x, y, preferred_element_type=F32)


def window_kernel(cells, cots, qkv_t, proj_t, up_t, down_t, gains, bias, label_col, label_row,
                  d_cells, g_qkv, g_proj, g_up, g_down, g_gain, table, probs_s):
    positions, head_count = bias.shape[:2]
    windows, _, features = cells.shape
    head_size = features // head_count
    factor = 1.0 / math.sqrt(head_size)
    for total in (g_qkv, g_proj, g_up, g_down, g_gain):
        total[...] = jnp.zeros(total.shape, F32)
    if windows > positions:
        table[...] = jnp.zeros(table.shape, F32)

    def body(w, carry):
        p = lax.rem(w, positions)
        gain_one, gain_two = gains[0:1].astype(F32), gains[1:2].astype(F32)
        lane_head = lax.broadcasted_iota(jnp.int32, (1, features), 1) // head_size
        heads = [(lane_head == h).astype(BF16) for h in range(head_count)]
        normed_one, inv_one = layer_norm(cells[w].astype(F32))
        scaled_one = (normed_one * gain_one).astype(BF16)
        q, k, v = (
            by_t(scaled_one, qkv_t[i * features : (i + 1) * features]).astype(BF16) for i in range(3)
        )
        same = label_col[p] == label_row[p]
        attended = jnp.zeros((WIN, features), F32)
        for h, head in enumerate(heads):
            scores = by_t(q * head, k) * factor + bias[p, h].astype(F32)
            scores = jnp.where(same, scores, -jnp.inf)
            raised = jnp.exp(scores - jnp.max(scores, axis=-1, keepdims=True))
            probs = raised * (1.0 / jnp.sum(raised, axis=-1, keepdims=True))
            probs_s[h] = probs
            attended = attended + plain(probs.astype(BF16), v * head)
        attended = attended.astype(BF16)
        middle = cells[w].astype(F32) + by_t(attended, proj_t[...])
        normed_two, inv_two = layer_norm(middle)
        scaled_two = (normed_two * gain_two).astype(BF16)
        cot = cots[w]
        activated, slope = gelu_pair(by_t(scaled_two, up_t[...]))
        g_down[...] += outer(cot, activated.astype(BF16))
        d_hidden = (plain(cot, down_t[...]) * slope).astype(BF16)
        g_up[...] += outer(d_hidden, scaled_two)
        d_htwo = plain(d_hidden, up_t[...])
        g_gain[1:2] += jnp.sum(d_htwo * normed_two, axis=0, keepdims=True)
        d_middle = cot.astype(F32) + norm_back(d_htwo * gain_two, normed_two, inv_two)
        d_middle_b = d_middle.astype(BF16)
        g_proj[...] += outer(d_middle_b, attended)
        d_att = plain(d_middle_b, proj_t[...]).astype(BF16)
        d_q, d_k, d_v = (jnp.zeros((WIN, features), F32) for _ in range(3))
        for h, head in enumerate(heads):
            probs, d_att_h = probs_s[h], d_att * head
            d_prob = by_t(d_att_h, v)
            d_v = d_v + outer(probs.astype(BF16), d_att_h)
            d_score = probs * (d_prob - jnp.sum(probs * d_prob, axis=-1, keepdims=True))
            if windows > positions:
                table[p, h] += d_score
            else:
                table[p, h] = d_score.astype(table.dtype)
            d_score_b = d_score.astype(BF16)
            d_q = d_q + plain(d_score_b, k * head)
            d_k = d_k + outer(d_score_b, q * head)
        d_hone = jnp.zeros((WIN, features), F32)
        for i, part in enumerate((d_q * factor, d_k * factor, d_v)):
            part = part.astype(BF16)
            span = slice(i * features, (i + 1) * features)
            g_qkv[span] += outer(part, scaled_one)
            d_hone = d_hone + plain(part, qkv_t[span])
        g_gain[0:1] += jnp.sum(d_hone * normed_one, axis=0, keepdims=True)
        d_cells[w] = (d_middle + norm_back(d_hone * gain_one, normed_one, inv_one)).astype(BF16)
        return carry

    lax.fori_loop(0, windows, body, 0)


def block_grads(cells, cots, qkv_t, proj_t, up_t, down_t, gains, bias, labels):
    features = cells.shape[1]
    positions, head_count = bias.shape[:2]
    windows = cells.shape[0] // WIN
    vmem = pl.BlockSpec(memory_space=pltpu.VMEM)
    outs = [((windows, WIN, features), BF16)]
    outs += [(w.shape, F32) for w in (qkv_t, proj_t, up_t, down_t)] + [((2, features), F32)]
    outs += [(bias.shape, F32 if windows > positions else BF16)]
    d_cells, *grads = pl.pallas_call(
        window_kernel,
        out_shape=[jax.ShapeDtypeStruct(*o) for o in outs],
        in_specs=[vmem] * 10,
        out_specs=[vmem] * len(outs),
        scratch_shapes=[pltpu.VMEM((head_count, WIN, WIN), F32)],
        compiler_params=pltpu.CompilerParams(vmem_limit_bytes=48 * 2**20),
    )(
        cells.reshape(windows, WIN, features), cots.reshape(windows, WIN, features),
        qkv_t, proj_t, up_t, down_t, gains, bias, labels[:, :, None], labels[:, None, :],
    )
    return (d_cells.reshape(cells.shape), *grads)


def shards(inputs, cotangent, qkv_weight, proj_weight, up_weight, down_weight, norm_gains, bias_table, type_of, region):
    levels, rows, cols, features = inputs.shape
    nlat, nlon = lax.axis_size("lat"), lax.axis_size("lon")
    level_windows, row_windows = levels // WPL, rows // WLAT
    type_count, head_count, part = bias_table.shape
    positions = level_windows * row_windows
    lat_index = lax.axis_index("lat")
    row_half, col_half, level_shift = WLAT // 2, WLON // 2, WPL // 2
    all_types = type_of.reshape(level_windows, nlat, row_windows).transpose(1, 0, 2).reshape(nlat, positions)
    types = lax.dynamic_index_in_dim(all_types, lat_index, 0, keepdims=False)
    n_up, n_qkv, n_proj = up_weight.shape[1], qkv_weight.shape[1], proj_weight.shape[1]
    gain_cols, height = norm_gains.shape[1], -(-max(n_up + 2, n_qkv + n_proj) // 8) * 8
    gain_rows = jnp.pad(norm_gains, ((0, height - n_up - 2), (0, features - gain_cols)))
    a_part = jnp.stack(
        [
            jnp.concatenate([up_weight.T, gain_rows]),
            jnp.pad(
                jnp.concatenate([qkv_weight.T, proj_weight.T]), ((0, height - n_qkv - n_proj), (0, 0))
            ),
        ]
    )
    d_part = down_weight.reshape(2, -1, down_weight.shape[1]).transpose(0, 2, 1)
    b_part = jnp.concatenate(
        [lax.dynamic_index_in_dim(bias_table, types[i], 0, keepdims=False) for i in range(positions)], axis=0
    )
    both = jnp.roll(jnp.stack([inputs, cotangent]), -level_shift, axis=1)
    rim_lat = both[:, :, :row_half, col_half:]
    rim_lon = both[:, :, row_half:, :col_half]
    rim_diag = both[:, :, :row_half, :col_half]
    flat = [r.reshape(-1, features) for r in (rim_lat, rim_lon, rim_diag)]
    dma = pltpu.SemaphoreType.DMA
    a_all, d_all, b_all, r_lat, r_lon, r_diag = comm_call(
        functools.partial(gather_kernel, nlat, nlon),
        0,
        [((nlon,) + x.shape, BF16) for x in (a_part, d_part, b_part)] + [(x.shape, BF16) for x in flat],
        [dma((3, nlon // 2))] * 4 + [dma((2, nlon))] * 2 + [dma((3,))] * 2,
        (a_part, d_part, b_part, *flat),
    )
    up_t = a_all[:, 0, :n_up].reshape(-1, features)
    qkv_t = a_all[:, 1, :n_qkv].reshape(-1, features)
    proj_t = a_all[:, 1, n_qkv : n_qkv + n_proj].reshape(-1, features)
    gains = a_all[:, 0, n_up : n_up + 2, :gain_cols].transpose(1, 0, 2).reshape(2, features)
    down_t = d_all.transpose(0, 2, 1, 3).reshape(features, -1)
    bias = b_all.transpose(1, 0, 2).reshape(positions, head_count, WIN, WIN)
    top = jnp.concatenate([both[:, :, row_half:, col_half:], r_lon.reshape(rim_lon.shape)], axis=3)
    bottom = jnp.concatenate([r_lat.reshape(rim_lat.shape), r_diag.reshape(rim_diag.shape)], axis=3)
    shifted = jnp.concatenate([top, bottom], axis=2)
    labels = region.reshape(level_windows, WPL, row_windows, WLAT).transpose(0, 2, 1, 3)
    labels = jnp.broadcast_to(labels[..., None], labels.shape + (WLON,)).reshape(positions, WIN)
    d_cells, g_qkv_t, g_proj_t, g_up_t, g_down_t, g_gains, table = block_grads(
        to_windows(shifted[0]), to_windows(shifted[1]), qkv_t, proj_t, up_t, down_t, gains, bias, labels
    )
    g_gain_rows = g_gains.reshape(2, nlon, gain_cols).transpose(1, 0, 2)
    g_gain_rows = jnp.pad(g_gain_rows, ((0, 0), (0, height - n_up - 2), (0, features - gain_cols)))
    g_up_t, g_qkv_t, g_proj_t = (g.reshape(nlon, -1, features) for g in (g_up_t, g_qkv_t, g_proj_t))
    ga = jnp.stack(
        [
            jnp.concatenate([g_up_t, g_gain_rows], axis=1),
            jnp.pad(
                jnp.concatenate([g_qkv_t, g_proj_t], axis=1), ((0, 0), (0, height - n_qkv - n_proj), (0, 0))
            ),
        ]
    ).astype(BF16)
    gd = g_down_t.reshape(nlon, -1, 2, g_down_t.shape[1] // 2).transpose(2, 0, 1, 3).astype(BF16)
    gt = table.astype(BF16).reshape(positions * head_count, nlon, part).transpose(1, 0, 2)
    onehot = (all_types[:, None, :] == jnp.arange(type_count, dtype=jnp.int32)[None, :, None]).astype(BF16)
    kron = jnp.einsum("lyp,gh->lygph", onehot, jnp.eye(head_count, dtype=BF16)).reshape(
        nlat, type_count * head_count, positions * head_count
    )
    back = from_windows(d_cells, levels, rows, cols)
    out_lat = back[:, rows - row_half :, : cols - col_half]
    out_lon = back[:, : rows - row_half, cols - col_half :]
    out_diag = back[:, rows - row_half :, cols - col_half :]
    flat = [r.reshape(-1, features) for r in (out_lat, out_lon, out_diag)]
    shard_shapes = (ga.shape[2:], gd.shape[2:], gt.shape[1:])
    token_count = levels * rows * cols * nlat * nlon
    a_sum, d_sum, t_sum, r_lat, r_lon, r_diag = comm_call(
        functools.partial(reduce_kernel, nlat, nlon, 1.0 / math.sqrt(token_count)),
        1,
        [((2,) + ga.shape[2:], F32), ((2,) + gd.shape[2:], F32), ((type_count * head_count, part), F32)]
        + [(x.shape, BF16) for x in flat],
        [pltpu.VMEM(x.shape[1:], BF16) for x in (ga, gd)] * 2
        + [pltpu.VMEM((nlon // 2,) + shape, BF16) for shape in shard_shapes] * 3
        + [pltpu.VMEM((nlat // 2,) + shape, BF16) for shape in shard_shapes[:2]]
        + [pltpu.VMEM((nlat,) + shard_shapes[2], BF16)]
        + [dma((2,))] * 2 + [dma((3, nlon // 2))] * 4 + [dma((3, nlat // 2))] * 4 + [dma((3,))] * 2,
        (ga, gd, gt, kron, *flat),
    )
    own = back[:, : rows - row_half, : cols - col_half]
    top = jnp.concatenate([r_diag.reshape(out_diag.shape), r_lat.reshape(out_lat.shape)], axis=2)
    bottom = jnp.concatenate([r_lon.reshape(out_lon.shape), own], axis=2)
    grad_input = jnp.roll(jnp.concatenate([top, bottom], axis=1), level_shift, axis=0)
    return (
        grad_input,
        a_sum[1, :n_qkv].T,
        a_sum[1, n_qkv : n_qkv + n_proj].T,
        a_sum[0, :n_up].T,
        d_sum.transpose(0, 2, 1).reshape(down_weight.shape),
        a_sum[0, n_up : n_up + 2, :gain_cols],
        t_sum.reshape(type_count, head_count, part),
    )


def solution(mesh):
    return jax.shard_map(
        shards,
        mesh=mesh,
        in_specs=(
            P(None, "lat", "lon", None),
            P(None, "lat", "lon", None),
            P(None, "lon"),
            P(None, "lon"),
            P(None, "lon"),
            P(None, "lon"),
            P(None, "lon"),
            P(None, None, "lon"),
            P(),
            P(None, "lat"),
        ),
        out_specs=(
            P(None, "lat", "lon", None),
            P(None, "lon"),
            P(None, "lon"),
            P(None, "lon"),
            P(None, "lon"),
            P(None, "lon"),
            P(None, None, "lon"),
        ),
        check_vma=False,
    )
```

```python
import functools
import math

import jax
import jax.numpy as jnp
from jax import lax
from jax.experimental import pallas as pl
from jax.experimental.pallas import tpu as pltpu
from jax.sharding import PartitionSpec as P

WPL = 2
WLAT = 6
WLON = 12
WIN = 144
MESH = pl.DeviceIdType.MESH
F32 = jnp.float32
BF16 = jnp.bfloat16


def layer_norm(values):
    row_mean = jnp.mean(values, axis=-1, keepdims=True)
    centred = values - row_mean
    variance = jnp.mean(centred * centred, axis=-1, keepdims=True)
    inv_std = lax.rsqrt(variance + 1e-05)
    return (centred * inv_std, inv_std)


def norm_back(d_normed, normed, inv_std):
    return inv_std * (
        d_normed
        - jnp.mean(d_normed, axis=-1, keepdims=True)
        - normed * jnp.mean(d_normed * normed, axis=-1, keepdims=True)
    )


def gelu_pair(pre_act):
    cumul = 0.5 * (1.0 + lax.erf(pre_act * 0.7071067811865476))
    density = jnp.exp(-0.5 * pre_act * pre_act) * 0.3989422804014327
    return (pre_act * cumul, cumul + pre_act * density)


def position(nlat, nlon):
    lat, lon = lax.axis_index("lat"), lax.axis_index("lon")

    def at(dlat, dlon):
        return (lax.rem(lat + dlat + nlat, nlat), lax.rem(lon + dlon + nlon, nlon))

    core, side = lax.rem(lat, 2), lax.rem(lon, 2)
    twin = (lat + 1 - 2 * core, lon)
    across = (lat, lon + 1 - 2 * side)
    return lat, lon, at, core, twin, across


def greet(devices):
    barrier = pltpu.get_barrier_semaphore()
    for device in devices:
        pl.semaphore_signal(barrier, inc=1, device_id=device, device_id_type=MESH)
    pl.semaphore_wait(barrier, len(devices))


def peers(nlat, nlon, at, twin, across):
    steps = [(0, d) for d in range(2, nlon, 2)] + [(d, 0) for d in range(2, nlat, 2)]
    steps += [(1, 0), (-1, 0), (0, 1), (0, -1), (1, 1), (-1, -1)]
    return [twin, across] + [at(*step) for step in steps]


def send(src, dst, send_sem, recv_sem, device):
    copy = pltpu.make_async_remote_copy(
        src_ref=src, dst_ref=dst, send_sem=send_sem, recv_sem=recv_sem, device_id=device, device_id_type=MESH
    )
    copy.start()
    return copy


def gather_kernel(nlat, nlon, a, d, b, h_lat, h_lon, h_diag, a_all, d_all, b_all, r_lat, r_lon, r_diag,
                  zs, zr, xs, xr, ts, tr, hs, hr):
    lat, lon, at, core, twin, across = position(nlat, nlon)
    greet(peers(nlat, nlon, at, twin, across))
    reach = nlon // 2
    srcs = (a.at[core], d.at[core], b)

    def slots(owner):
        return (a_all.at[owner, core], d_all.at[owner, core], b_all.at[owner])

    far, near, shared, halo = {}, {}, [], []
    for k in range(1, reach):
        for i in range(3):
            far[i, k] = send(srcs[i], slots(lon)[i], zs.at[i, k], zr.at[i, k], at(0, 2 * k))
    for i in range(3):
        near[i, 0] = send(srcs[i], slots(lon)[i], xs.at[i, 0], xr.at[i, 0], across)
    for i, (src, dst, step) in enumerate(
        ((h_lat, r_lat, (-1, 0)), (h_lon, r_lon, (0, -1)), (h_diag, r_diag, (-1, -1)))
    ):
        halo.append(send(src, dst, hs.at[i], hr.at[i], at(*step)))
    a_all[lon] = a[...]
    d_all[lon] = d[...]
    b_all[lon] = b[...]
    for k in range(1, reach):
        owner = lax.rem(lon - 2 * k + nlon, nlon)
        for i in range(3):
            slot = slots(owner)[i]
            far[i, k].wait_recv()
            near[i, k] = send(slot, slot, xs.at[i, k], xr.at[i, k], across)
            if i < 2:
                shared.append(send(slot, slot, ts.at[i, k], tr.at[i, k], twin))
    for k in range(reach):
        owner = lax.rem(across[1] - 2 * k + nlon, nlon)
        for i in range(3):
            slot = slots(owner)[i]
            near[i, k].wait_recv()
            if i < 2:
                shared.append(send(slot, slot, ts.at[i, reach + k], tr.at[i, reach + k], twin))
    for copy in list(far.values()) + list(near.values()):
        copy.wait_send()
    for copy in halo + shared:
        copy.wait()


def reduce_kernel(nlat, nlon, scale, a, d, t, kron, h_lat, h_lon, h_diag, a_out, d_out, t_out, r_lat, r_lon, r_diag,
                  a_twin, d_twin, a_half, d_half, a_x, d_x, t_x, a_mid, d_mid, t_mid, a_z, d_z, t_z,
                  a_row, d_row, t_row, cs, cr, xs, xr, zs, zr, ls, lr, fs, fr, hs, hr):
    lat, lon, at, core, twin, across = position(nlat, nlon)
    greet(peers(nlat, nlon, at, twin, across))
    reach = nlon // 2
    near, far, rest = {}, {}, []
    order = list(range(1, reach)) + [0]
    pairs = [
        send(src.at[1 - core], dst, cs.at[i], cr.at[i], twin)
        for i, (src, dst) in enumerate(((a, a_twin), (d, d_twin)))
    ]

    def cross(i, src, dst):
        for k in order:
            owner = lax.rem(across[1] + 2 * k, nlon)
            near[i, k] = send(src.at[owner], dst.at[k], xs.at[i, k], xr.at[i, k], across)

    cross(2, t, t_x)
    for i, (src, dst, step) in enumerate(
        ((h_lat, r_lat, (1, 0)), (h_lon, r_lon, (0, 1)), (h_diag, r_diag, (1, 1)))
    ):
        rest.append(send(src, dst, hs.at[i], hr.at[i], at(*step)))
    for i, (own, got, half, dst) in enumerate(((a, a_twin, a_half, a_x), (d, d_twin, d_half, d_x))):
        pairs[i].wait()
        half[...] = (own[core].astype(F32) + got[...].astype(F32)).astype(BF16)
        cross(i, half, dst)
    streams = ((2, t, t_x, t_mid, t_z), (0, a_half, a_x, a_mid, a_z), (1, d_half, d_x, d_mid, d_z))
    for i, own, got, mid, dst in streams:
        for k in range(1, reach):
            owner = lax.rem(lon + 2 * k, nlon)
            near[i, k].wait_recv()
            mid[k] = (own[owner].astype(F32) + got[k].astype(F32)).astype(BF16)
            far[i, k] = send(mid.at[k], dst.at[k], zs.at[i, k], zr.at[i, k], at(0, 2 * k))
    rows = nlat // 2
    row = lax.div(lat, 2)

    def total_of(i, own, got, dst):
        near[i, 0].wait_recv()
        total = own[lon].astype(F32) + got[0].astype(F32)
        for k in range(1, reach):
            far[i, k].wait_recv()
            total = total + dst[k].astype(F32)
        return total.astype(BF16)

    t_row[lat] = total_of(2, t, t_x, t_z)
    rest.append(send(t_row.at[lat], t_row.at[lat], ls.at[2, 0], lr.at[2, 0], twin))
    t_far = [send(t_row.at[lat], t_row.at[lat], ls.at[2, j], lr.at[2, j], at(2 * j, 0)) for j in range(1, rows)]
    halves = []
    for i, own, got, dst, line in ((0, a_half, a_x, a_z, a_row), (1, d_half, d_x, d_z, d_row)):
        line[row] = total_of(i, own, got, dst)
        halves.append(
            [send(line.at[row], line.at[row], ls.at[i, j], lr.at[i, j], at(2 * j, 0)) for j in range(1, rows)]
        )
    for j in range(1, rows):
        slot = t_row.at[lax.rem(lat - 2 * j + nlat, nlat)]
        t_far[j - 1].wait_recv()
        rest.append(send(slot, slot, fs.at[2, j], fr.at[2, j], twin))
    for i, (line, out) in enumerate(((a_row, a_out), (d_row, d_out))):
        for copy in halves[i]:
            copy.wait_recv()
        total = line[0].astype(F32)
        for j in range(1, rows):
            total = total + line[j].astype(F32)
        out[core] = total * scale
        rest.append(send(out.at[core], out.at[core], fs.at[i, 0], fr.at[i, 0], twin))
    for copy in list(near.values()) + list(far.values()) + t_far + halves[0] + halves[1]:
        copy.wait_send()
    for copy in rest:
        copy.wait()
    total = jnp.zeros(t_out.shape, F32)
    for i in range(nlat):
        total = total + jnp.dot(kron[i], t_row[i], preferred_element_type=F32)
    t_out[...] = total


def comm_call(kernel, collective_id, outs, scratch, operands):
    vmem = pl.BlockSpec(memory_space=pltpu.VMEM)
    return pl.pallas_call(
        kernel,
        out_shape=[jax.ShapeDtypeStruct(*o) for o in outs],
        in_specs=[vmem] * len(operands),
        out_specs=[vmem] * len(outs),
        scratch_shapes=scratch,
        compiler_params=pltpu.CompilerParams(
            collective_id=collective_id, has_side_effects=True, vmem_limit_bytes=48 * 2**20
        ),
    )(*operands)


def to_windows(grid):
    p, l, c = grid.shape[:3]
    shaped = grid.reshape(p // WPL, WPL, l // WLAT, WLAT, c // WLON, WLON, grid.shape[-1])
    return shaped.transpose(4, 0, 2, 1, 3, 5, 6).reshape(-1, grid.shape[-1])


def from_windows(flat, p, l, c):
    shaped = flat.reshape(c // WLON, p // WPL, l // WLAT, WPL, WLAT, WLON, flat.shape[-1])
    return shaped.transpose(1, 3, 2, 4, 0, 5, 6).reshape(p, l, c, flat.shape[-1])


def by_t(x, w_t):
    return lax.dot_general(x, w_t, (((1,), (1,)), ((), ())), preferred_element_type=F32)


def outer(x, y):
    return lax.dot_general(x, y, (((0,), (0,)), ((), ())), preferred_element_type=F32)


def plain(x, y):
    return jnp.dot(x, y, preferred_element_type=F32)


def pick_kernel(types, table, out):
    positions = types.shape[0]
    rows = [table[types[i]].astype(F32) for i in range(positions)]
    out[...] = jnp.concatenate(rows, axis=0).astype(BF16)


def pick_rows(types, table):
    _, head_count, part = table.shape
    return pl.pallas_call(
        pick_kernel,
        out_shape=jax.ShapeDtypeStruct((types.shape[0] * head_count, part), BF16),
        in_specs=[pl.BlockSpec(memory_space=pltpu.SMEM), pl.BlockSpec(memory_space=pltpu.VMEM)],
        out_specs=pl.BlockSpec(memory_space=pltpu.VMEM),
    )(types, table)


def window_kernel(n_up, n_qkv, n_proj, cells, cots, a_all, d_all, bias, label_col, label_row,
                  d_cells, ga, gd, table,
                  probs_s, qkv_t, proj_t, up_t, down_t, gains, g_qkv, g_proj, g_up, g_down, g_gain):
    owners, height = a_all.shape[0], a_all.shape[2]

    def joined(half, start, count):
        rows = [a_all[j, half].astype(F32)[start : start + count] for j in range(owners)]
        return jnp.concatenate(rows, axis=0).astype(BF16)

    up_t[...] = joined(0, 0, n_up)
    qkv_t[...] = joined(1, 0, n_qkv)
    proj_t[...] = joined(1, n_qkv, n_proj)
    wide = d_all.shape[3]
    for i in range(2):
        rows = [d_all[j, i].astype(F32) for j in range(owners)]
        down_t[:, i * wide : (i + 1) * wide] = jnp.concatenate(rows, axis=0).astype(BF16)
    gain_sum = a_all[0, 0].astype(F32)[n_up : n_up + 2]
    for j in range(1, owners):
        gain_sum = gain_sum + a_all[j, 0].astype(F32)[n_up : n_up + 2]
    gains[...] = gain_sum
    positions, head_count = bias.shape[:2]
    windows, _, features = cells.shape
    head_size = features // head_count
    factor = 1.0 / math.sqrt(head_size)
    for total in (g_qkv, g_proj, g_up, g_down, g_gain):
        total[...] = jnp.zeros(total.shape, F32)
    if windows > positions:
        table[...] = jnp.zeros(table.shape, F32)

    def body(w, carry):
        p = lax.rem(w, positions)
        gain_one, gain_two = gains[0:1], gains[1:2]
        lane_head = lax.broadcasted_iota(jnp.int32, (1, features), 1) // head_size
        heads = [(lane_head == h).astype(BF16) for h in range(head_count)]
        normed_one, inv_one = layer_norm(cells[w].astype(F32))
        scaled_one = (normed_one * gain_one).astype(BF16)
        q, k, v = (
            by_t(scaled_one, qkv_t[i * features : (i + 1) * features]).astype(BF16) for i in range(3)
        )
        same = label_col[p] == label_row[p]
        attended = jnp.zeros((WIN, features), F32)
        for h, head in enumerate(heads):
            scores = by_t(q * head, k) * factor + bias[p, h].astype(F32)
            scores = jnp.where(same, scores, -jnp.inf)
            raised = jnp.exp(scores - jnp.max(scores, axis=-1, keepdims=True))
            probs = raised * (1.0 / jnp.sum(raised, axis=-1, keepdims=True))
            probs_s[h] = probs
            attended = attended + plain(probs.astype(BF16), v * head)
        attended = attended.astype(BF16)
        middle = cells[w].astype(F32) + by_t(attended, proj_t[...])
        normed_two, inv_two = layer_norm(middle)
        scaled_two = (normed_two * gain_two).astype(BF16)
        cot = cots[w]
        activated, slope = gelu_pair(by_t(scaled_two, up_t[...]))
        g_down[...] += outer(cot, activated.astype(BF16))
        d_hidden = (plain(cot, down_t[...]) * slope).astype(BF16)
        g_up[...] += outer(d_hidden, scaled_two)
        d_htwo = plain(d_hidden, up_t[...])
        g_gain[1:2] += jnp.sum(d_htwo * normed_two, axis=0, keepdims=True)
        d_middle = cot.astype(F32) + norm_back(d_htwo * gain_two, normed_two, inv_two)
        d_middle_b = d_middle.astype(BF16)
        g_proj[...] += outer(d_middle_b, attended)
        d_att = plain(d_middle_b, proj_t[...]).astype(BF16)
        d_q, d_k, d_v = (jnp.zeros((WIN, features), F32) for _ in range(3))
        for h, head in enumerate(heads):
            probs, d_att_h = probs_s[h], d_att * head
            d_prob = by_t(d_att_h, v)
            d_v = d_v + outer(probs.astype(BF16), d_att_h)
            d_score = probs * (d_prob - jnp.sum(probs * d_prob, axis=-1, keepdims=True))
            if windows > positions:
                table[p, h] += d_score
            else:
                table[p, h] = d_score.astype(table.dtype)
            d_score_b = d_score.astype(BF16)
            d_q = d_q + plain(d_score_b, k * head)
            d_k = d_k + outer(d_score_b, q * head)
        d_hone = jnp.zeros((WIN, features), F32)
        for i, part in enumerate((d_q * factor, d_k * factor, d_v)):
            part = part.astype(BF16)
            span = slice(i * features, (i + 1) * features)
            g_qkv[span] += outer(part, scaled_one)
            d_hone = d_hone + plain(part, qkv_t[span])
        g_gain[0:1] += jnp.sum(d_hone * normed_one, axis=0, keepdims=True)
        d_cells[w] = (d_middle + norm_back(d_hone * gain_one, normed_one, inv_one)).astype(BF16)
        return carry

    lax.fori_loop(0, windows, body, 0)
    features = cells.shape[2]
    down = d_all.shape[2]
    gain_rows = jnp.concatenate([g_gain[...], jnp.zeros((height - n_up - 2, features), F32)], axis=0)
    spare = height - n_qkv - n_proj
    for j in range(owners):
        ga[0, j] = jnp.concatenate([g_up[j * n_up : (j + 1) * n_up], gain_rows], axis=0).astype(BF16)
        rows = [g_qkv[j * n_qkv : (j + 1) * n_qkv], g_proj[j * n_proj : (j + 1) * n_proj]]
        rows += [jnp.zeros((spare, features), F32)] if spare else []
        ga[1, j] = jnp.concatenate(rows, axis=0).astype(BF16)
        for i in range(2):
            gd[i, j] = g_down[j * down : (j + 1) * down, i * wide : (i + 1) * wide].astype(BF16)


def block_grads(cells, cots, a_all, d_all, cuts, bias, labels):
    features = cells.shape[1]
    positions, head_count = bias.shape[:2]
    windows, owners, wide = cells.shape[0] // WIN, a_all.shape[0], d_all.shape[3] * 2
    vmem = pl.BlockSpec(memory_space=pltpu.VMEM)
    outs = [((windows, WIN, features), BF16)]
    outs += [((2, owners) + x.shape[2:], BF16) for x in (a_all, d_all)]
    outs += [(bias.shape, F32 if windows > positions else BF16)]
    n_up, n_qkv, n_proj = cuts
    sizes = [(owners * n, features) for n in (n_qkv, n_proj, n_up)] + [(features, wide)]
    d_cells, *grads = pl.pallas_call(
        functools.partial(window_kernel, *cuts),
        out_shape=[jax.ShapeDtypeStruct(*o) for o in outs],
        in_specs=[vmem] * 7,
        out_specs=[vmem] * len(outs),
        scratch_shapes=[pltpu.VMEM((head_count, WIN, WIN), F32)]
        + [pltpu.VMEM(size, BF16) for size in sizes] + [pltpu.VMEM((2, features), F32)]
        + [pltpu.VMEM(size, F32) for size in sizes] + [pltpu.VMEM((2, features), F32)],
        compiler_params=pltpu.CompilerParams(vmem_limit_bytes=48 * 2**20),
    )(
        cells.reshape(windows, WIN, features), cots.reshape(windows, WIN, features),
        a_all, d_all, bias, labels[:, :, None], labels[:, None, :],
    )
    return (d_cells.reshape(cells.shape), *grads)


def shards(inputs, cotangent, qkv_weight, proj_weight, up_weight, down_weight, norm_gains, bias_table, type_of, region):
    levels, rows, cols, features = inputs.shape
    nlat, nlon = lax.axis_size("lat"), lax.axis_size("lon")
    level_windows, row_windows = levels // WPL, rows // WLAT
    type_count, head_count, part = bias_table.shape
    positions = level_windows * row_windows
    lat_index = lax.axis_index("lat")
    row_half, col_half, level_shift = WLAT // 2, WLON // 2, WPL // 2
    all_types = type_of.reshape(level_windows, nlat, row_windows).transpose(1, 0, 2).reshape(nlat, positions)
    types = lax.dynamic_index_in_dim(all_types, lat_index, 0, keepdims=False)
    n_up, n_qkv, n_proj = up_weight.shape[1], qkv_weight.shape[1], proj_weight.shape[1]
    gain_cols, height = norm_gains.shape[1], -(-max(n_up + 2, n_qkv + n_proj) // 8) * 8
    gain_spot = lax.axis_index("lon") * gain_cols
    gain_rows = lax.dynamic_update_slice(
        jnp.zeros((height - n_up, features), BF16), norm_gains, (jnp.int32(0), gain_spot)
    )
    a_part = jnp.stack(
        [
            jnp.concatenate([up_weight.T, gain_rows]),
            jnp.pad(
                jnp.concatenate([qkv_weight.T, proj_weight.T]), ((0, height - n_qkv - n_proj), (0, 0))
            ),
        ]
    )
    d_part = down_weight.reshape(2, -1, down_weight.shape[1]).transpose(0, 2, 1)
    b_part = pick_rows(types, bias_table)
    both = jnp.roll(jnp.stack([inputs, cotangent]), -level_shift, axis=1)
    rim_lat = both[:, :, :row_half, col_half:]
    rim_lon = both[:, :, row_half:, :col_half]
    rim_diag = both[:, :, :row_half, :col_half]
    flat = [r.reshape(-1, features) for r in (rim_lat, rim_lon, rim_diag)]
    dma = pltpu.SemaphoreType.DMA
    a_all, d_all, b_all, r_lat, r_lon, r_diag = comm_call(
        functools.partial(gather_kernel, nlat, nlon),
        0,
        [((nlon,) + x.shape, BF16) for x in (a_part, d_part, b_part)] + [(x.shape, BF16) for x in flat],
        [dma((3, nlon // 2))] * 4 + [dma((2, nlon))] * 2 + [dma((3,))] * 2,
        (a_part, d_part, b_part, *flat),
    )
    bias = b_all.transpose(1, 0, 2).reshape(positions, head_count, WIN, WIN)
    top = jnp.concatenate([both[:, :, row_half:, col_half:], r_lon.reshape(rim_lon.shape)], axis=3)
    bottom = jnp.concatenate([r_lat.reshape(rim_lat.shape), r_diag.reshape(rim_diag.shape)], axis=3)
    shifted = jnp.concatenate([top, bottom], axis=2)
    labels = region.reshape(level_windows, WPL, row_windows, WLAT).transpose(0, 2, 1, 3)
    labels = jnp.broadcast_to(labels[..., None], labels.shape + (WLON,)).reshape(positions, WIN)
    d_cells, ga, gd, table = block_grads(
        to_windows(shifted[0]), to_windows(shifted[1]), a_all, d_all, (n_up, n_qkv, n_proj), bias, labels
    )
    gt = table.astype(BF16).reshape(positions * head_count, nlon, part).transpose(1, 0, 2)
    onehot = (all_types[:, None, :] == jnp.arange(type_count, dtype=jnp.int32)[None, :, None]).astype(BF16)
    kron = jnp.einsum("lyp,gh->lygph", onehot, jnp.eye(head_count, dtype=BF16)).reshape(
        nlat, type_count * head_count, positions * head_count
    )
    back = from_windows(d_cells, levels, rows, cols)
    out_lat = back[:, rows - row_half :, : cols - col_half]
    out_lon = back[:, : rows - row_half, cols - col_half :]
    out_diag = back[:, rows - row_half :, cols - col_half :]
    flat = [r.reshape(-1, features) for r in (out_lat, out_lon, out_diag)]
    shard_shapes = (ga.shape[2:], gd.shape[2:], gt.shape[1:])
    token_count = levels * rows * cols * nlat * nlon
    a_sum, d_sum, t_sum, r_lat, r_lon, r_diag = comm_call(
        functools.partial(reduce_kernel, nlat, nlon, 1.0 / math.sqrt(token_count)),
        1,
        [((2,) + ga.shape[2:], F32), ((2,) + gd.shape[2:], F32), ((type_count * head_count, part), F32)]
        + [(x.shape, BF16) for x in flat],
        [pltpu.VMEM(x.shape[1:], BF16) for x in (ga, gd)] * 2
        + [pltpu.VMEM((nlon // 2,) + shape, BF16) for shape in shard_shapes] * 3
        + [pltpu.VMEM((nlat // 2,) + shape, BF16) for shape in shard_shapes[:2]]
        + [pltpu.VMEM((nlat,) + shard_shapes[2], BF16)]
        + [dma((2,))] * 2 + [dma((3, nlon // 2))] * 4 + [dma((3, nlat // 2))] * 4 + [dma((3,))] * 2,
        (ga, gd, gt, kron, *flat),
    )
    own = back[:, : rows - row_half, : cols - col_half]
    top = jnp.concatenate([r_diag.reshape(out_diag.shape), r_lat.reshape(out_lat.shape)], axis=2)
    bottom = jnp.concatenate([r_lon.reshape(out_lon.shape), own], axis=2)
    grad_input = jnp.roll(jnp.concatenate([top, bottom], axis=1), level_shift, axis=0)
    return (
        grad_input,
        a_sum[1, :n_qkv].T,
        a_sum[1, n_qkv : n_qkv + n_proj].T,
        a_sum[0, :n_up].T,
        d_sum.transpose(0, 2, 1).reshape(down_weight.shape),
        lax.dynamic_slice(a_sum[0, n_up : n_up + 2], (jnp.int32(0), gain_spot), (2, gain_cols)),
        t_sum.reshape(type_count, head_count, part),
    )


def solution(mesh):
    return jax.shard_map(
        shards,
        mesh=mesh,
        in_specs=(
            P(None, "lat", "lon", None),
            P(None, "lat", "lon", None),
            P(None, "lon"),
            P(None, "lon"),
            P(None, "lon"),
            P(None, "lon"),
            P(None, "lon"),
            P(None, None, "lon"),
            P(),
            P(None, "lat"),
        ),
        out_specs=(
            P(None, "lat", "lon", None),
            P(None, "lon"),
            P(None, "lon"),
            P(None, "lon"),
            P(None, "lon"),
            P(None, "lon"),
            P(None, None, "lon"),
        ),
        check_vma=False,
    )
```

```python
import functools
import math

import jax
import jax.numpy as jnp
from jax import lax
from jax.experimental import pallas as pl
from jax.experimental.pallas import tpu as pltpu
from jax.sharding import PartitionSpec as P

WPL = 2
WLAT = 6
WLON = 12
WIN = 144
MESH = pl.DeviceIdType.MESH
F32 = jnp.float32
BF16 = jnp.bfloat16


def layer_norm(values):
    row_mean = jnp.mean(values, axis=-1, keepdims=True)
    centred = values - row_mean
    variance = jnp.mean(centred * centred, axis=-1, keepdims=True)
    inv_std = lax.rsqrt(variance + 1e-05)
    return (centred * inv_std, inv_std)


def norm_back(d_normed, normed, inv_std):
    return inv_std * (
        d_normed
        - jnp.mean(d_normed, axis=-1, keepdims=True)
        - normed * jnp.mean(d_normed * normed, axis=-1, keepdims=True)
    )


def gelu_pair(pre_act):
    cumul = 0.5 * (1.0 + lax.erf(pre_act * 0.7071067811865476))
    density = jnp.exp(-0.5 * pre_act * pre_act) * 0.3989422804014327
    return (pre_act * cumul, cumul + pre_act * density)


def position(nlat, nlon):
    lat, lon = lax.axis_index("lat"), lax.axis_index("lon")

    def at(dlat, dlon):
        return (lax.rem(lat + dlat + nlat, nlat), lax.rem(lon + dlon + nlon, nlon))

    core, side = lax.rem(lat, 2), lax.rem(lon, 2)
    twin = (lat + 1 - 2 * core, lon)
    across = (lat, lon + 1 - 2 * side)
    return lat, lon, at, core, twin, across


def greet(devices):
    barrier = pltpu.get_barrier_semaphore()
    for device in devices:
        pl.semaphore_signal(barrier, inc=1, device_id=device, device_id_type=MESH)
    pl.semaphore_wait(barrier, len(devices))


def peers(nlat, nlon, at, twin, across):
    steps = [(0, d) for d in range(2, nlon, 2)] + [(d, 0) for d in range(2, nlat, 2)]
    steps += [(1, 0), (-1, 0), (0, 1), (0, -1), (1, 1), (-1, -1)]
    return [twin, across] + [at(*step) for step in steps]


def send(src, dst, send_sem, recv_sem, device):
    copy = pltpu.make_async_remote_copy(
        src_ref=src, dst_ref=dst, send_sem=send_sem, recv_sem=recv_sem, device_id=device, device_id_type=MESH
    )
    copy.start()
    return copy


def gather_kernel(nlat, nlon, a, d, b, h_lat, h_lon, h_diag, a_all, d_all, b_all, r_lat, r_lon, r_diag,
                  zs, zr, xs, xr, ts, tr, hs, hr):
    lat, lon, at, core, twin, across = position(nlat, nlon)
    greet(peers(nlat, nlon, at, twin, across))
    reach = nlon // 2
    srcs = (a.at[core], d.at[core], b)

    def slots(owner):
        return (a_all.at[owner, core], d_all.at[owner, core], b_all.at[owner])

    far, near, shared, halo = {}, {}, [], []
    for k in range(1, reach):
        for i in range(3):
            far[i, k] = send(srcs[i], slots(lon)[i], zs.at[i, k], zr.at[i, k], at(0, 2 * k))
    for i in range(3):
        near[i, 0] = send(srcs[i], slots(lon)[i], xs.at[i, 0], xr.at[i, 0], across)
    for i, (src, dst, step) in enumerate(
        ((h_lat, r_lat, (-1, 0)), (h_lon, r_lon, (0, -1)), (h_diag, r_diag, (-1, -1)))
    ):
        halo.append(send(src, dst, hs.at[i], hr.at[i], at(*step)))
    a_all[lon] = a[...]
    d_all[lon] = d[...]
    b_all[lon] = b[...]
    for k in range(1, reach):
        owner = lax.rem(lon - 2 * k + nlon, nlon)
        for i in range(3):
            slot = slots(owner)[i]
            far[i, k].wait_recv()
            near[i, k] = send(slot, slot, xs.at[i, k], xr.at[i, k], across)
            if i < 2:
                shared.append(send(slot, slot, ts.at[i, k], tr.at[i, k], twin))
    for k in range(reach):
        owner = lax.rem(across[1] - 2 * k + nlon, nlon)
        for i in range(3):
            slot = slots(owner)[i]
            near[i, k].wait_recv()
            if i < 2:
                shared.append(send(slot, slot, ts.at[i, reach + k], tr.at[i, reach + k], twin))
    for copy in list(far.values()) + list(near.values()):
        copy.wait_send()
    for copy in halo + shared:
        copy.wait()


def reduce_kernel(nlat, nlon, scale, a, d, t, kron, h_lat, h_lon, h_diag, a_out, d_out, t_out, r_lat, r_lon, r_diag,
                  a_twin, d_twin, a_half, d_half, a_x, d_x, t_x, a_mid, d_mid, t_mid, a_z, d_z, t_z,
                  a_row, d_row, t_row, cs, cr, xs, xr, zs, zr, ls, lr, fs, fr, hs, hr):
    lat, lon, at, core, twin, across = position(nlat, nlon)
    greet(peers(nlat, nlon, at, twin, across))
    reach = nlon // 2
    near, far, rest = {}, {}, []
    order = list(range(1, reach)) + [0]
    pairs = [
        send(src.at[1 - core], dst, cs.at[i], cr.at[i], twin)
        for i, (src, dst) in enumerate(((a, a_twin), (d, d_twin)))
    ]

    def cross(i, src, dst):
        for k in order:
            owner = lax.rem(across[1] + 2 * k, nlon)
            near[i, k] = send(src.at[owner], dst.at[k], xs.at[i, k], xr.at[i, k], across)

    cross(2, t, t_x)
    for i, (src, dst, step) in enumerate(
        ((h_lat, r_lat, (1, 0)), (h_lon, r_lon, (0, 1)), (h_diag, r_diag, (1, 1)))
    ):
        rest.append(send(src, dst, hs.at[i], hr.at[i], at(*step)))
    for i, (own, got, half, dst) in enumerate(((a, a_twin, a_half, a_x), (d, d_twin, d_half, d_x))):
        pairs[i].wait()
        half[...] = (own[core].astype(F32) + got[...].astype(F32)).astype(BF16)
        cross(i, half, dst)
    streams = ((2, t, t_x, t_mid, t_z), (0, a_half, a_x, a_mid, a_z), (1, d_half, d_x, d_mid, d_z))
    for i, own, got, mid, dst in streams:
        for k in range(1, reach):
            owner = lax.rem(lon + 2 * k, nlon)
            near[i, k].wait_recv()
            mid[k] = (own[owner].astype(F32) + got[k].astype(F32)).astype(BF16)
            far[i, k] = send(mid.at[k], dst.at[k], zs.at[i, k], zr.at[i, k], at(0, 2 * k))
    rows = nlat // 2
    row = lax.div(lat, 2)

    def total_of(i, own, got, dst):
        near[i, 0].wait_recv()
        total = own[lon].astype(F32) + got[0].astype(F32)
        for k in range(1, reach):
            far[i, k].wait_recv()
            total = total + dst[k].astype(F32)
        return total.astype(BF16)

    t_row[lat] = total_of(2, t, t_x, t_z)
    rest.append(send(t_row.at[lat], t_row.at[lat], ls.at[2, 0], lr.at[2, 0], twin))
    t_far = [send(t_row.at[lat], t_row.at[lat], ls.at[2, j], lr.at[2, j], at(2 * j, 0)) for j in range(1, rows)]
    halves = []
    for i, own, got, dst, line in ((0, a_half, a_x, a_z, a_row), (1, d_half, d_x, d_z, d_row)):
        line[row] = total_of(i, own, got, dst)
        halves.append(
            [send(line.at[row], line.at[row], ls.at[i, j], lr.at[i, j], at(2 * j, 0)) for j in range(1, rows)]
        )
    for j in range(1, rows):
        slot = t_row.at[lax.rem(lat - 2 * j + nlat, nlat)]
        t_far[j - 1].wait_recv()
        rest.append(send(slot, slot, fs.at[2, j], fr.at[2, j], twin))
    for i, (line, out) in enumerate(((a_row, a_out), (d_row, d_out))):
        for copy in halves[i]:
            copy.wait_recv()
        total = line[0].astype(F32)
        for j in range(1, rows):
            total = total + line[j].astype(F32)
        out[core] = total * scale
        rest.append(send(out.at[core], out.at[core], fs.at[i, 0], fr.at[i, 0], twin))
    for copy in list(near.values()) + list(far.values()) + t_far + halves[0] + halves[1]:
        copy.wait_send()
    for copy in rest:
        copy.wait()
    total = jnp.zeros(t_out.shape, F32)
    for i in range(nlat):
        total = total + jnp.dot(kron[i], t_row[i], preferred_element_type=F32)
    t_out[...] = total


def comm_call(kernel, collective_id, outs, scratch, operands):
    vmem = pl.BlockSpec(memory_space=pltpu.VMEM)
    return pl.pallas_call(
        kernel,
        out_shape=[jax.ShapeDtypeStruct(*o) for o in outs],
        in_specs=[vmem] * len(operands),
        out_specs=[vmem] * len(outs),
        scratch_shapes=scratch,
        compiler_params=pltpu.CompilerParams(
            collective_id=collective_id, has_side_effects=True, vmem_limit_bytes=48 * 2**20
        ),
    )(*operands)


def to_windows(grid):
    p, l, c = grid.shape[:3]
    shaped = grid.reshape(p // WPL, WPL, l // WLAT, WLAT, c // WLON, WLON, grid.shape[-1])
    return shaped.transpose(4, 0, 2, 1, 3, 5, 6).reshape(-1, grid.shape[-1])


def from_windows(flat, p, l, c):
    shaped = flat.reshape(c // WLON, p // WPL, l // WLAT, WPL, WLAT, WLON, flat.shape[-1])
    return shaped.transpose(1, 3, 2, 4, 0, 5, 6).reshape(p, l, c, flat.shape[-1])


def by_t(x, w_t):
    return lax.dot_general(x, w_t, (((1,), (1,)), ((), ())), preferred_element_type=F32)


def outer(x, y):
    return lax.dot_general(x, y, (((0,), (0,)), ((), ())), preferred_element_type=F32)


def plain(x, y):
    return jnp.dot(x, y, preferred_element_type=F32)


def pick_kernel(types, table, out):
    positions = types.shape[0]
    rows = [table[types[i]].astype(F32) for i in range(positions)]
    out[...] = jnp.concatenate(rows, axis=0).astype(BF16)


def pick_rows(types, table):
    _, head_count, part = table.shape
    return pl.pallas_call(
        pick_kernel,
        out_shape=jax.ShapeDtypeStruct((types.shape[0] * head_count, part), BF16),
        in_specs=[pl.BlockSpec(memory_space=pltpu.SMEM), pl.BlockSpec(memory_space=pltpu.VMEM)],
        out_specs=pl.BlockSpec(memory_space=pltpu.VMEM),
    )(types, table)


def window_kernel(n_up, n_qkv, n_proj, cells, cots, a_all, d_all, bias, label_col, label_row,
                  d_cells, ga, gd, table,
                  probs_s, qkv_t, proj_t, up_t, down_t, gains, g_qkv, g_proj, g_up, g_down, g_gain):
    owners, height = a_all.shape[0], a_all.shape[2]

    def joined(half, start, count):
        rows = [a_all[j, half].astype(F32)[start : start + count] for j in range(owners)]
        return jnp.concatenate(rows, axis=0).astype(BF16)

    up_t[...] = joined(0, 0, n_up)
    qkv_t[...] = joined(1, 0, n_qkv)
    proj_t[...] = joined(1, n_qkv, n_proj)
    wide = d_all.shape[3]
    for i in range(2):
        rows = [d_all[j, i].astype(F32) for j in range(owners)]
        down_t[:, i * wide : (i + 1) * wide] = jnp.concatenate(rows, axis=0).astype(BF16)
    gain_sum = a_all[0, 0].astype(F32)[n_up : n_up + 2]
    for j in range(1, owners):
        gain_sum = gain_sum + a_all[j, 0].astype(F32)[n_up : n_up + 2]
    gains[...] = gain_sum
    positions, head_count = bias.shape[:2]
    windows, _, features = cells.shape
    head_size = features // head_count
    factor = 1.0 / math.sqrt(head_size)
    for total in (g_qkv, g_proj, g_up, g_down, g_gain):
        total[...] = jnp.zeros(total.shape, F32)
    if windows > positions:
        table[...] = jnp.zeros(table.shape, F32)

    def body(w, carry):
        p = lax.rem(w, positions)
        gain_one, gain_two = gains[0:1], gains[1:2]
        lane_head = lax.broadcasted_iota(jnp.int32, (1, features), 1) // head_size
        heads = [(lane_head == h).astype(BF16) for h in range(head_count)]
        normed_one, inv_one = layer_norm(cells[w].astype(F32))
        scaled_one = (normed_one * gain_one).astype(BF16)
        q, k, v = (
            by_t(scaled_one, qkv_t[i * features : (i + 1) * features]).astype(BF16) for i in range(3)
        )
        same = label_col[p] == label_row[p]
        attended = jnp.zeros((WIN, features), F32)
        for h, head in enumerate(heads):
            scores = by_t(q * head, k) * factor + bias[p, h].astype(F32)
            scores = jnp.where(same, scores, -jnp.inf)
            raised = jnp.exp(scores - jnp.max(scores, axis=-1, keepdims=True))
            probs = raised * (1.0 / jnp.sum(raised, axis=-1, keepdims=True))
            probs_s[h] = probs
            attended = attended + plain(probs.astype(BF16), v * head)
        attended = attended.astype(BF16)
        middle = cells[w].astype(F32) + by_t(attended, proj_t[...])
        normed_two, inv_two = layer_norm(middle)
        scaled_two = (normed_two * gain_two).astype(BF16)
        cot = cots[w]
        activated, slope = gelu_pair(by_t(scaled_two, up_t[...]))
        g_down[...] += outer(cot, activated.astype(BF16))
        d_hidden = (plain(cot, down_t[...]) * slope).astype(BF16)
        g_up[...] += outer(d_hidden, scaled_two)
        d_htwo = plain(d_hidden, up_t[...])
        g_gain[1:2] += jnp.sum(d_htwo * normed_two, axis=0, keepdims=True)
        d_middle = cot.astype(F32) + norm_back(d_htwo * gain_two, normed_two, inv_two)
        d_middle_b = d_middle.astype(BF16)
        g_proj[...] += outer(d_middle_b, attended)
        d_att = plain(d_middle_b, proj_t[...]).astype(BF16)
        d_q, d_k, d_v = (jnp.zeros((WIN, features), F32) for _ in range(3))
        for h, head in enumerate(heads):
            probs, d_att_h = probs_s[h], d_att * head
            d_prob = by_t(d_att_h, v)
            d_v = d_v + outer(probs.astype(BF16), d_att_h)
            d_score = probs * (d_prob - jnp.sum(probs * d_prob, axis=-1, keepdims=True))
            if windows > positions:
                table[p, h] += d_score
            else:
                table[p, h] = d_score.astype(table.dtype)
            d_score_b = d_score.astype(BF16)
            d_q = d_q + plain(d_score_b, k * head)
            d_k = d_k + outer(d_score_b, q * head)
        d_hone = jnp.zeros((WIN, features), F32)
        for i, part in enumerate((d_q * factor, d_k * factor, d_v)):
            part = part.astype(BF16)
            span = slice(i * features, (i + 1) * features)
            g_qkv[span] += outer(part, scaled_one)
            d_hone = d_hone + plain(part, qkv_t[span])
        g_gain[0:1] += jnp.sum(d_hone * normed_one, axis=0, keepdims=True)
        d_cells[w] = (d_middle + norm_back(d_hone * gain_one, normed_one, inv_one)).astype(BF16)
        return carry

    lax.fori_loop(0, windows, body, 0)
    features = cells.shape[2]
    down = d_all.shape[2]
    gain_rows = jnp.concatenate([g_gain[...], jnp.zeros((height - n_up - 2, features), F32)], axis=0)
    spare = height - n_qkv - n_proj
    for j in range(owners):
        ga[0, j] = jnp.concatenate([g_up[j * n_up : (j + 1) * n_up], gain_rows], axis=0).astype(BF16)
        rows = [g_qkv[j * n_qkv : (j + 1) * n_qkv], g_proj[j * n_proj : (j + 1) * n_proj]]
        rows += [jnp.zeros((spare, features), F32)] if spare else []
        ga[1, j] = jnp.concatenate(rows, axis=0).astype(BF16)
        for i in range(2):
            gd[i, j] = g_down[j * down : (j + 1) * down, i * wide : (i + 1) * wide].astype(BF16)


def block_grads(cells, cots, a_all, d_all, cuts, bias, labels):
    features = cells.shape[1]
    positions, head_count = bias.shape[:2]
    windows, owners, wide = cells.shape[0] // WIN, a_all.shape[0], d_all.shape[3] * 2
    vmem = pl.BlockSpec(memory_space=pltpu.VMEM)
    outs = [((windows, WIN, features), BF16)]
    outs += [((2, owners) + x.shape[2:], BF16) for x in (a_all, d_all)]
    outs += [(bias.shape, F32 if windows > positions else BF16)]
    n_up, n_qkv, n_proj = cuts
    sizes = [(owners * n, features) for n in (n_qkv, n_proj, n_up)] + [(features, wide)]
    d_cells, *grads = pl.pallas_call(
        functools.partial(window_kernel, *cuts),
        out_shape=[jax.ShapeDtypeStruct(*o) for o in outs],
        in_specs=[vmem] * 7,
        out_specs=[vmem] * len(outs),
        scratch_shapes=[pltpu.VMEM((head_count, WIN, WIN), F32)]
        + [pltpu.VMEM(size, BF16) for size in sizes] + [pltpu.VMEM((2, features), F32)]
        + [pltpu.VMEM(size, F32) for size in sizes] + [pltpu.VMEM((2, features), F32)],
        compiler_params=pltpu.CompilerParams(vmem_limit_bytes=48 * 2**20),
    )(
        cells.reshape(windows, WIN, features), cots.reshape(windows, WIN, features),
        a_all, d_all, bias, labels[:, :, None], labels[:, None, :],
    )
    return (d_cells.reshape(cells.shape), *grads)


def shards(inputs, cotangent, qkv_weight, proj_weight, up_weight, down_weight, norm_gains, bias_table, type_of, region):
    levels, rows, cols, features = inputs.shape
    nlat, nlon = lax.axis_size("lat"), lax.axis_size("lon")
    level_windows, row_windows = levels // WPL, rows // WLAT
    type_count, head_count, part = bias_table.shape
    positions = level_windows * row_windows
    lat_index = lax.axis_index("lat")
    row_half, col_half, level_shift = WLAT // 2, WLON // 2, WPL // 2
    all_types = type_of.reshape(level_windows, nlat, row_windows).transpose(1, 0, 2).reshape(nlat, positions)
    types = lax.dynamic_index_in_dim(all_types, lat_index, 0, keepdims=False)
    n_up, n_qkv, n_proj = up_weight.shape[1], qkv_weight.shape[1], proj_weight.shape[1]
    gain_cols, height = norm_gains.shape[1], -(-max(n_up + 2, n_qkv + n_proj) // 8) * 8
    gain_spot = lax.axis_index("lon") * gain_cols
    own_lane = jnp.arange(features, dtype=jnp.int32) // gain_cols == lax.axis_index("lon")
    gain_rows = jnp.where(own_lane, jnp.tile(norm_gains, (1, nlon)), jnp.zeros((), BF16))
    gain_rows = jnp.pad(gain_rows, ((0, height - n_up - 2), (0, 0)))
    a_part = jnp.stack(
        [
            jnp.concatenate([up_weight.T, gain_rows]),
            jnp.pad(
                jnp.concatenate([qkv_weight.T, proj_weight.T]), ((0, height - n_qkv - n_proj), (0, 0))
            ),
        ]
    )
    d_part = down_weight.reshape(2, -1, down_weight.shape[1]).transpose(0, 2, 1)
    b_part = pick_rows(types, bias_table)
    both = jnp.roll(jnp.stack([inputs, cotangent]), -level_shift, axis=1)
    rim_lat = both[:, :, :row_half, col_half:]
    rim_lon = both[:, :, row_half:, :col_half]
    rim_diag = both[:, :, :row_half, :col_half]
    flat = [r.reshape(-1, features) for r in (rim_lat, rim_lon, rim_diag)]
    dma = pltpu.SemaphoreType.DMA
    a_all, d_all, b_all, r_lat, r_lon, r_diag = comm_call(
        functools.partial(gather_kernel, nlat, nlon),
        0,
        [((nlon,) + x.shape, BF16) for x in (a_part, d_part, b_part)] + [(x.shape, BF16) for x in flat],
        [dma((3, nlon // 2))] * 4 + [dma((2, nlon))] * 2 + [dma((3,))] * 2,
        (a_part, d_part, b_part, *flat),
    )
    bias = b_all.transpose(1, 0, 2).reshape(positions, head_count, WIN, WIN)
    top = jnp.concatenate([both[:, :, row_half:, col_half:], r_lon.reshape(rim_lon.shape)], axis=3)
    bottom = jnp.concatenate([r_lat.reshape(rim_lat.shape), r_diag.reshape(rim_diag.shape)], axis=3)
    shifted = jnp.concatenate([top, bottom], axis=2)
    labels = region.reshape(level_windows, WPL, row_windows, WLAT).transpose(0, 2, 1, 3)
    labels = jnp.broadcast_to(labels[..., None], labels.shape + (WLON,)).reshape(positions, WIN)
    d_cells, ga, gd, table = block_grads(
        to_windows(shifted[0]), to_windows(shifted[1]), a_all, d_all, (n_up, n_qkv, n_proj), bias, labels
    )
    gt = table.astype(BF16).reshape(positions * head_count, nlon, part).transpose(1, 0, 2)
    onehot = (all_types[:, None, :] == jnp.arange(type_count, dtype=jnp.int32)[None, :, None]).astype(BF16)
    kron = jnp.einsum("lyp,gh->lygph", onehot, jnp.eye(head_count, dtype=BF16)).reshape(
        nlat, type_count * head_count, positions * head_count
    )
    back = from_windows(d_cells, levels, rows, cols)
    out_lat = back[:, rows - row_half :, : cols - col_half]
    out_lon = back[:, : rows - row_half, cols - col_half :]
    out_diag = back[:, rows - row_half :, cols - col_half :]
    flat = [r.reshape(-1, features) for r in (out_lat, out_lon, out_diag)]
    shard_shapes = (ga.shape[2:], gd.shape[2:], gt.shape[1:])
    token_count = levels * rows * cols * nlat * nlon
    a_sum, d_sum, t_sum, r_lat, r_lon, r_diag = comm_call(
        functools.partial(reduce_kernel, nlat, nlon, 1.0 / math.sqrt(token_count)),
        1,
        [((2,) + ga.shape[2:], F32), ((2,) + gd.shape[2:], F32), ((type_count * head_count, part), F32)]
        + [(x.shape, BF16) for x in flat],
        [pltpu.VMEM(x.shape[1:], BF16) for x in (ga, gd)] * 2
        + [pltpu.VMEM((nlon // 2,) + shape, BF16) for shape in shard_shapes] * 3
        + [pltpu.VMEM((nlat // 2,) + shape, BF16) for shape in shard_shapes[:2]]
        + [pltpu.VMEM((nlat,) + shard_shapes[2], BF16)]
        + [dma((2,))] * 2 + [dma((3, nlon // 2))] * 4 + [dma((3, nlat // 2))] * 4 + [dma((3,))] * 2,
        (ga, gd, gt, kron, *flat),
    )
    own = back[:, : rows - row_half, : cols - col_half]
    top = jnp.concatenate([r_diag.reshape(out_diag.shape), r_lat.reshape(out_lat.shape)], axis=2)
    bottom = jnp.concatenate([r_lon.reshape(out_lon.shape), own], axis=2)
    grad_input = jnp.roll(jnp.concatenate([top, bottom], axis=1), level_shift, axis=0)
    return (
        grad_input,
        a_sum[1, :n_qkv].T,
        a_sum[1, n_qkv : n_qkv + n_proj].T,
        a_sum[0, :n_up].T,
        d_sum.transpose(0, 2, 1).reshape(down_weight.shape),
        lax.dynamic_slice(a_sum[0, n_up : n_up + 2], (jnp.int32(0), gain_spot), (2, gain_cols)),
        t_sum.reshape(type_count, head_count, part),
    )


def solution(mesh):
    return jax.shard_map(
        shards,
        mesh=mesh,
        in_specs=(
            P(None, "lat", "lon", None),
            P(None, "lat", "lon", None),
            P(None, "lon"),
            P(None, "lon"),
            P(None, "lon"),
            P(None, "lon"),
            P(None, "lon"),
            P(None, None, "lon"),
            P(),
            P(None, "lat"),
        ),
        out_specs=(
            P(None, "lat", "lon", None),
            P(None, "lon"),
            P(None, "lon"),
            P(None, "lon"),
            P(None, "lon"),
            P(None, "lon"),
            P(None, None, "lon"),
        ),
        check_vma=False,
    )
```
